32 devices in a mesh: arc: 2 (over y), trow: 4 (over z), tcol: 4 (over x, core).
Axes of the slice: x: 2, y: 2, z: 4, core: 2. Of those that a mesh axis runs over, the one named last changes fastest.
Arguments:
- design: bfloat16 [1280, 8192], P('arc', 'tcol'), may hold values from -0.25 to 0.25
- local_design: bfloat16 [1280, 128], P('arc'), may hold values from -0.3125 to 0.3125
- lengths: int32 [4], P('arc'), may hold values from 1 to 320, 960 in all
- regularizer: float32 [8192], P(('arc', 'trow')), may hold values from 0.2 to 2
Outputs:
- normal: float32 [8192, 8192], P(('arc', 'trow'), 'tcol')
- panel_factor: float32 [2, 8192, 512], P(None, 'tcol')
The draws below stay inside these ranges and needn't reach their ends.
Inputs may be any that keep to these rules, and one draw needn't show every extreme that they name: `lengths`: each arc has at least one live row; some arc is full.
All inputs are finite; a program needn't handle non-finite values. No bound on the sum of `lengths` on one device may be relied on, other than what follows from the above.
Results may differ from the reference program's by a relative error of at most 0.003.
Values may be sent and summed in bfloat16 or wider, within the bound.
No kernel may reach another device: no remote copies, remote signals or barrier semaphores. Data moves between devices by JAX's collectives and lax.ppermute only.
A program may use at most 128 MiB of HBM per device.

```python
import math
import jax
import jax.numpy as jnp
import numpy as np
from jax import lax

G = 8192
LOCAL = 128
PANEL = 512
PANELS = 2
CAP = 320
ARCS = 4
ROWS = 1280


def strengthened(result, rng, source, target, blocks, factor):
    def block_of(position):
        return (jnp.arange(result.shape[position]) // (result.shape[position] // blocks)).reshape((-1,) + (1,) * (result.ndim - 1 - position))

    one_side = jax.random.permutation(rng, blocks)[block_of(target)]
    second = (block_of(target) + blocks // 2) % blocks
    return jnp.where((block_of(source) == one_side) | (block_of(source) == second), factor * result, result)


def block_scale(key, extent, split, smallest, largest):
    level, own = 1.0, jax.random.fold_in(key, 6)
    for position, blocks in split:
        steps = jnp.exp(jax.random.uniform(jax.random.fold_in(own, position), (blocks,), jnp.float32, smallest / len(split), largest / len(split)))
        level = level * jnp.repeat(steps, extent[position] // blocks).reshape([-1 if axis == position else 1 for axis in range(len(extent))])
    return level


def profile(amount, total, bound, lean):
    loads = [(1 << 20) // math.isqrt(standing ** lean) + 1 for standing in range(2, amount + 1)]
    surplus, given = total - bound - (amount - 1), [1] * (amount - 1)
    while surplus > 0:
        free = [i for i in range(amount - 1) if given[i] < bound]
        pool, remaining = sum([loads[i] for i in free]), surplus
        for i in free:
            extra = min(bound - given[i], max(1, remaining * loads[i] // pool), surplus)
            given[i] = given[i] + extra
            surplus = surplus - extra
    return np.array([bound] + given)


def uneven_parts(rng, amount, total, reach, slope):
    if amount == 2:
        one = jax.random.randint(rng, (), max(1, total - reach), min(reach, total - 1) + 1)
        return jnp.stack([one, total - one])
    sizes = jnp.asarray(profile(amount, total, reach, slope), jnp.int32)
    pairs = (amount - 1) // 2
    source_of, sink = sizes[1:1 + 2 * pairs:2], sizes[2:2 + 2 * pairs:2]
    margin = jnp.minimum(source_of - 1, reach - sink)
    shifted = jax.random.randint(jax.random.fold_in(rng, 1), (pairs,), 0, 1 << 20) % (margin + 1)
    sizes = sizes.at[1:1 + 2 * pairs:2].set(source_of - shifted).at[2:2 + 2 * pairs:2].set(sink + shifted)
    return sizes[jax.random.permutation(jax.random.fold_in(rng, 2), amount)]


def noise(key, dims, scale, most, shards=(), kind=jnp.bfloat16):
    gain = block_scale(key, dims, shards, -0.22, 0.18) if shards else 1.0
    values = jax.random.normal(key, dims, jnp.float32) * scale * gain
    return jnp.minimum(jnp.maximum(values, -most), most).astype(kind)


def noise_with(key, extent, scale, bound, cuts, heavy, kind=jnp.bfloat16):
    array = scale * jax.random.normal(key, extent, jnp.float32)
    if cuts:
        array = array * block_scale(key, extent, cuts, -0.22, 0.18)
    return jnp.clip(strengthened(array, jax.random.fold_in(key, 3), *heavy), -bound, bound).astype(kind)


def setup_inputs(seed: int = 0) -> dict:
    key_list = jax.random.split(jax.random.key(seed), 5)
    return {
        "design": noise_with(key_list[0], (ROWS, G), ROWS ** -0.5, 0.25, ((0, 2), (1, 4)), (0, 1, 4, 2.0)),
        "local_design": noise(key_list[1], (ROWS, LOCAL), CAP ** -0.5, 0.3125, ((0, 2),)),
        "lengths": uneven_parts(key_list[2], ARCS, ARCS * CAP * 3 // 4, CAP, 2).astype(jnp.int32),
        "regularizer": jnp.clip(jnp.exp(math.log(2.0) - 2.3025851 * jax.random.uniform(key_list[3], (G,), jnp.float32) ** block_scale(key_list[3], (G,), ((0, 8),), -0.2, 0.2)), 0.2, 2.0),
    }


ridge = 0.1

def reference(design, local_design, lengths, regularizer):
    arc_blocks = design.reshape(ARCS, CAP, G)
    local_cols = local_design.reshape(ARCS, CAP, LOCAL)
    live_rows = jnp.arange(CAP, dtype=jnp.int32)[None, :] < lengths[:, None]
    arc_blocks = jnp.where(live_rows[:, :, None], arc_blocks, jnp.zeros((), design.dtype))
    local_cols = jnp.where(live_rows[:, :, None], local_cols, jnp.zeros((), local_design.dtype)).astype(jnp.float32)
    local_normal = jnp.einsum('acl,acm->alm', local_cols, local_cols)
    local_normal = local_normal + ridge * jnp.eye(LOCAL, dtype=jnp.float32)[None]
    local_factor = jnp.linalg.cholesky(local_normal)
    basis_rows = lax.linalg.triangular_solve(local_factor, jnp.transpose(local_cols, (0, 2, 1)), left_side=True, lower=True)
    basis_rows = basis_rows.astype(jnp.bfloat16)
    basis_wide = basis_rows.astype(jnp.float32)
    loadings = jnp.einsum('alc,acw->alw', basis_wide, arc_blocks.astype(jnp.float32)).astype(jnp.bfloat16)
    cleaned = arc_blocks.astype(jnp.float32) - jnp.einsum('alc,alw->acw', basis_wide, loadings.astype(jnp.float32))
    flat_rows = cleaned.astype(jnp.bfloat16).reshape(ROWS, G)
    normal_work = jnp.dot(flat_rows.T.astype(jnp.float32), flat_rows.astype(jnp.float32), preferred_element_type=jnp.float32) + jnp.diag(regularizer)
    row_ids = jnp.arange(G, dtype=jnp.int32)
    panel_factors = []
    for panel_index in range(PANELS):
        lead_col = panel_index * PANEL
        panel_strip = normal_work[lead_col:lead_col + PANEL, :]
        lower_factor = jnp.linalg.cholesky(panel_strip[:, lead_col:lead_col + PANEL])
        col_factor = lax.linalg.triangular_solve(lower_factor, panel_strip, left_side=True, lower=True).T
        col_factor = jnp.where(row_ids[:, None] >= lead_col, col_factor, jnp.zeros((), jnp.float32))
        normal_work = normal_work - jnp.dot(col_factor, col_factor.T, precision=lax.Precision.HIGHEST)
        panel_factors.append(col_factor)
    return (normal_work, jnp.stack(panel_factors))
```

```python
import jax
import jax.numpy as jnp
from jax import lax
from jax.sharding import PartitionSpec as P

PANEL = 512
PANELS = 2
AXES = ("arc", "trow", "tcol")

ridge = 0.1

HIGHEST = lax.Precision.HIGHEST


class Plan:
    def __init__(self, mesh):
        self.arc, self.trow, self.tcol = (mesh.shape[name] for name in AXES)

    def flat(self, arc, trow, tcol):
        return (arc * self.trow + trow) * self.tcol + tcol

    def devices(self):
        for arc in range(self.arc):
            for trow in range(self.trow):
                for tcol in range(self.tcol):
                    yield arc, trow, tcol

    def shift_arc(self, block, step, keep=None):
        pairs = [
            (self.flat(a, r, c), self.flat((a + step) % self.arc, r, c))
            for a, r, c in self.devices()
            if keep is None or keep(a, r, c)
        ]
        return lax.ppermute(block, AXES, pairs)

    def gather_arc(self, block, keep=None):
        return [block] + [self.shift_arc(block, s, keep) for s in range(1, self.arc)]

    def spread_tcol(self, block, holder):
        me = lax.axis_index("tcol")
        offsets = [0]
        index = lax.axis_index("arc") * self.trow + lax.axis_index("trow")
        table = jnp.array(
            [holder(a, r) for a in range(self.arc) for r in range(self.trow)], jnp.int32
        )
        offset = me ^ table[index]
        span = self.tcol // 2
        while span:
            pairs = [
                (self.flat(a, r, holder(a, r) ^ o), self.flat(a, r, holder(a, r) ^ o ^ span))
                for a in range(self.arc)
                for r in range(self.trow)
                for o in offsets
            ]
            got = lax.ppermute(block, AXES, pairs)
            received = (offset & (2 * span - 1)) == span
            block = jnp.where(received, got, block)
            offsets = offsets + [o ^ span for o in offsets]
            span //= 2
        return block

    def order_arcs(self, pieces):
        stacked = jnp.stack(pieces)
        if self.arc == 1:
            return stacked
        me = lax.axis_index("arc")
        return jnp.take(stacked, (me - jnp.arange(self.arc)) % self.arc, axis=0)

    def gather_rows(self, tile):
        me = lax.axis_index("arc") * self.trow + lax.axis_index("trow")
        total = self.arc * self.trow
        span = 1
        while span < total:
            pairs = [
                (self.flat(a, r, c), self.flat((t ^ span) // self.trow, (t ^ span) % self.trow, c))
                for a, r, c in self.devices()
                for t in [a * self.trow + r]
            ]
            got = lax.ppermute(tile, AXES, pairs)
            low = (me & span) == 0
            tile = jnp.concatenate([jnp.where(low, tile, got), jnp.where(low, got, tile)])
            span *= 2
        return tile


def local_basis(local_half):
    local_normal = jnp.einsum(
        "acl,acm->alm", local_half, local_half, preferred_element_type=jnp.float32
    )
    local_normal = local_normal + ridge * jnp.eye(local_half.shape[2], dtype=jnp.float32)[None]
    local_factor = jnp.linalg.cholesky(local_normal)
    local_cols = local_half.astype(jnp.float32)
    basis_rows = lax.linalg.triangular_solve(
        local_factor, jnp.transpose(local_cols, (0, 2, 1)), left_side=True, lower=True
    )
    return basis_rows.astype(jnp.bfloat16)


def project(blocks, basis):
    loadings = jnp.einsum(
        "alc,acw->alw", basis, blocks, preferred_element_type=jnp.float32
    ).astype(jnp.bfloat16)
    cleaned = blocks.astype(jnp.float32) - jnp.einsum(
        "alc,alw->acw", basis, loadings, preferred_element_type=jnp.float32
    )
    cleaned = cleaned.astype(jnp.bfloat16)
    return cleaned.reshape(-1, cleaned.shape[2])


def contract_rows(left_rows, right_rows):
    return lax.dot_general(
        left_rows, right_rows, (((0,), (0,)), ((), ())), preferred_element_type=jnp.float32
    )


def per_device(plan, design, local_design, lengths, regularizer):
    row_count, col_width = design.shape
    tile_rows = regularizer.shape[0]
    own_arcs = lengths.shape[0]
    capacity = row_count // own_arcs
    tile_index = lax.axis_index("arc") * plan.trow + lax.axis_index("trow")
    row_start = tile_index * tile_rows
    col_start = lax.axis_index("tcol") * col_width
    lead = PANEL * PANELS

    live_rows = jnp.arange(capacity, dtype=jnp.int32)[None, :] < lengths[:, None]
    live_flat = live_rows.reshape(row_count, 1)
    masked = jnp.where(live_flat, design, jnp.zeros((), design.dtype))
    local_half = local_design.reshape(own_arcs, capacity, -1)
    local_half = jnp.where(live_rows[:, :, None], local_half, jnp.zeros((), local_design.dtype))

    lead_own = masked[:, :lead]
    lead_pieces = [
        plan.spread_tcol(piece, lambda a, r: 0)
        for piece in plan.gather_arc(lead_own, lambda a, r, c: c == 0)
    ]
    col_pieces = plan.gather_arc(masked)

    def tile_holder(a, r):
        return (a * plan.trow + r) * tile_rows // col_width

    tile_offset = lax.rem(row_start, col_width)
    row_pieces = [
        plan.spread_tcol(
            lax.dynamic_slice_in_dim(piece, tile_offset, tile_rows, 1), tile_holder
        )
        for piece in col_pieces
    ]
    all_regularizer = plan.gather_rows(regularizer)

    basis_own = local_basis(local_half)
    basis = plan.order_arcs(plan.gather_arc(basis_own)).reshape(-1, *basis_own.shape[1:])

    def whole(pieces):
        blocks = plan.order_arcs(pieces)
        return blocks.reshape(-1, capacity, blocks.shape[-1])

    lead_rows = project(whole(lead_pieces), basis)
    pivot = contract_rows(lead_rows, lead_rows) + jnp.diag(all_regularizer[:lead])

    cols_global = col_start + jnp.arange(col_width, dtype=jnp.int32)
    rows_global = row_start + jnp.arange(tile_rows, dtype=jnp.int32)
    both_global = jnp.concatenate([cols_global, rows_global])
    col_rows = project(whole(col_pieces), basis)
    tile_cols = project(whole(row_pieces), basis)
    both = jnp.concatenate([col_rows, tile_cols], axis=1)
    strips = contract_rows(lead_rows, both)
    lead_ids = jnp.arange(lead, dtype=jnp.int32)
    strips = strips + jnp.where(
        lead_ids[:, None] == both_global[None, :],
        all_regularizer[:lead, None],
        jnp.zeros((), jnp.float32),
    )
    normal_block = contract_rows(tile_cols, col_rows)
    normal_block = normal_block + jnp.where(
        rows_global[:, None] == cols_global[None, :],
        regularizer[:, None],
        jnp.zeros((), jnp.float32),
    )
    panel_factors = []
    for panel in range(PANELS):
        lower = jnp.linalg.cholesky(pivot[:PANEL, :PANEL])
        wide = jnp.concatenate([pivot[:PANEL, PANEL:], strips[:PANEL]], axis=1)
        solved = lax.linalg.triangular_solve(lower, wide, left_side=True, lower=True)
        left = pivot.shape[1] - PANEL
        ahead, factor = solved[:, :left], solved[:, left:]
        factor = jnp.where(
            both_global[None, :] >= panel * PANEL, factor, jnp.zeros((), jnp.float32)
        )
        panel_factors.append(factor)
        if left:
            pivot = pivot[PANEL:, PANEL:] - lax.dot_general(
                ahead, ahead, (((0,), (0,)), ((), ())), precision=HIGHEST
            )
            strips = strips[PANEL:] - lax.dot_general(
                ahead, factor, (((0,), (0,)), ((), ())), precision=HIGHEST
            )
    stacked = jnp.concatenate(panel_factors)
    normal_block = normal_block - lax.dot_general(
        stacked[:, col_width:],
        stacked[:, :col_width],
        (((0,), (0,)), ((), ())),
        precision=HIGHEST,
    )
    outs = jnp.stack([jnp.transpose(f[:, :col_width]) for f in panel_factors])
    return (normal_block, outs)


def solution(mesh):
    plan = Plan(mesh)

    def body(*args):
        return per_device(plan, *args)

    return jax.shard_map(
        body,
        mesh=mesh,
        in_specs=(P("arc", "tcol"), P("arc", None), P("arc"), P(("arc", "trow"))),
        out_specs=(P(("arc", "trow"), "tcol"), P(None, "tcol", None)),
        check_vma=False,
    )
```

```python
import functools

import jax
import jax.numpy as jnp
import numpy as np
from jax import lax
from jax.experimental import pallas as pl
from jax.experimental.pallas import tpu as pltpu
from jax.sharding import PartitionSpec as P

PANEL = 512
PANELS = 2
AXES = ("arc", "trow", "tcol")
CORES = 2
WIDTH = 1024


ridge = 0.1

HIGHEST = lax.Precision.HIGHEST
LANES = 128
SUB = 8


def inverse_factor(rows_list):
    groups = LANES // SUB
    lane = lax.broadcasted_iota(jnp.int32, (SUB, LANES), 1)
    sub = lax.broadcasted_iota(jnp.int32, (SUB, LANES), 0)
    outs = [[] for _ in rows_list]
    state = [list(rows) for rows in rows_list]
    for s in range(groups):
        j = s * SUB
        inside = (lane >= j) & (lane < j + SUB)
        for b, rows in enumerate(state):
            lead = rows[s]
            unit = jnp.where(lane == sub + j, 1.0, 0.0)
            merged = jnp.where(inside, unit, lead)
            z = [jnp.broadcast_to(merged[k:k + 1, :], (SUB, LANES)) for k in range(SUB)]
            sp = {
                (m, k): jnp.broadcast_to(lead[k:k + 1, j + m:j + m + 1], (SUB, LANES))
                for k in range(SUB) for m in range(k, SUB)
            }
            below = list(range(s + 1, groups))
            col = {
                (t, k): jnp.broadcast_to(rows[t][:, j + k:j + k + 1], (SUB, LANES))
                for t in below for k in range(SUB)
            }
            rest = {t: jnp.where(inside, 0.0, rows[t]) for t in below}
            for k in range(SUB):
                inv = lax.rsqrt(sp[k, k])
                z[k] = z[k] * inv
                l = {m: sp[m, k] * inv for m in range(k + 1, SUB)}
                for m in range(k + 1, SUB):
                    for n in range(m, SUB):
                        sp[n, m] = sp[n, m] - l[n] * l[m]
                for m in range(k + 1, SUB):
                    z[m] = z[m] - l[m] * z[k]
                for t in below:
                    c = col[t, k] * inv
                    for m in range(k + 1, SUB):
                        col[t, m] = col[t, m] - c * l[m]
                    rest[t] = rest[t] - c * z[k]
            for t in below:
                rows[t] = rest[t]
            done = z[0]
            for k in range(1, SUB):
                done = jnp.where(sub == k, z[k], done)
            outs[b].append(jnp.where(lane <= sub + j, done, 0.0))
    return outs


def rows_of(block):
    return [block[SUB * t:SUB * (t + 1), :] for t in range(LANES // SUB)]


class Plan:
    def __init__(self, mesh):
        self.arc, self.trow, self.tcol = (mesh.shape[name] for name in AXES)
        self.across = self.tcol // CORES

    def flat(self, arc, trow, tcol):
        return (arc % self.arc * self.trow + trow) * self.tcol + tcol % self.tcol

    def move(self, block, arcs, across, source=None):
        pairs = [
            (self.flat(a, r, c), self.flat(a + arcs, r, c + across * CORES))
            for a in range(self.arc)
            for r in range(self.trow)
            for c in range(self.tcol)
            if source is None or source(a, r, c)
        ]
        return lax.ppermute(block, AXES, pairs)

    def core_swap(self, block):
        pairs = [
            (self.flat(a, r, c), self.flat(a, r, c ^ 1))
            for a in range(self.arc)
            for r in range(self.trow)
            for c in range(self.tcol)
        ]
        return lax.ppermute(block, AXES, pairs)

    def own_half(self, block, holder_core):
        half = block.shape[0] // CORES
        core = lax.axis_index("tcol") % CORES
        got = self.core_swap(block)
        mine = lax.dynamic_slice_in_dim(block, core * half, half, 0)
        theirs = lax.dynamic_slice_in_dim(got, core * half, half, 0)
        return jnp.where(core == holder_core, mine, theirs)

    def gather_rows(self, tile):
        me = lax.axis_index("arc") * self.trow + lax.axis_index("trow")
        total = self.arc * self.trow
        span = 1
        while span < total:
            pairs = [
                (t * self.tcol + c, (t ^ span) * self.tcol + c)
                for t in range(total)
                for c in range(self.tcol)
            ]
            got = lax.ppermute(tile, AXES, pairs)
            low = (me & span) == 0
            tile = jnp.concatenate([jnp.where(low, tile, got), jnp.where(low, got, tile)])
            span *= 2
        return tile


def local_kernel(a_ref, n_ref):
    count = a_ref.shape[0]
    found = inverse_factor([rows_of(a_ref[b]) for b in range(count)])
    for b in range(count):
        n_ref[b] = jnp.concatenate(found[b], axis=0)


def local_call(a):
    return pl.pallas_call(
        local_kernel,
        out_shape=jax.ShapeDtypeStruct(a.shape, jnp.float32),
        in_specs=[pl.BlockSpec(memory_space=pltpu.VMEM)],
        out_specs=pl.BlockSpec(memory_space=pltpu.VMEM),
        name="local_inverse",
    )(a)


def local_basis(local_half):
    local_normal = jnp.einsum(
        "acl,acm->alm", local_half, local_half, preferred_element_type=jnp.float32
    )
    local_normal = local_normal + ridge * jnp.eye(local_half.shape[2], dtype=jnp.float32)[None]
    inverse = local_call(local_normal)
    basis_rows = jnp.einsum(
        "alm,acm->alc", inverse, local_half.astype(jnp.float32), precision=HIGHEST
    )
    return basis_rows.astype(jnp.bfloat16)


def after(value, *earlier):
    return lax.optimization_barrier((value,) + earlier)[0]


def product(left, right, dims, precision=None):
    return lax.dot_general(
        left, right, (dims, ((), ())), precision=precision, preferred_element_type=jnp.float32
    )


def fine(left, right, dims):
    left_top, right_top = left.astype(jnp.bfloat16), right.astype(jnp.bfloat16)
    left_rest = (left - left_top.astype(jnp.float32)).astype(jnp.bfloat16)
    right_rest = (right - right_top.astype(jnp.float32)).astype(jnp.bfloat16)
    return product(left_top, right_top, dims) + (
        product(left_top, right_rest, dims) + product(left_rest, right_top, dims)
    )


def project_kernel(firsts, where_ref, *refs):
    basis_ref, turned_ref, out_ref = refs[-3], refs[-2], refs[-1]
    step = pl.program_id(0)

    def clean(block):
        loadings = product(basis_ref[0], block, ((1,), (0,))).astype(jnp.bfloat16)
        cleaned = block.astype(jnp.float32) - product(turned_ref[0], loadings, ((1,), (0,)))
        out_ref[...] = cleaned.astype(jnp.bfloat16)

    for piece, first in enumerate(firsts):
        last = firsts[piece + 1] if piece + 1 < len(firsts) else pl.num_programs(0)

        @pl.when((step >= first) & (step < last))
        def _(ref=refs[piece]):
            clean(ref[...])


def project(pieces, bases, arc_count, width):
    basis, turned = bases
    capacity = basis.shape[2]
    tile = min(WIDTH, min(block.shape[1] for block, *_ in pieces))
    firsts, steps = [], []
    for piece, (block, *_) in enumerate(pieces):
        firsts.append(len(steps))
        for a in range(block.shape[0] // capacity):
            for j in range(block.shape[1] // tile):
                steps.append((piece, a, j))
    total = len(steps)
    table = np.zeros((3, total), np.int32)
    table[0] = [a for _, a, _ in steps]
    table[1] = [a for _, a, _ in steps]
    table[2] = [j for _, _, j in steps]
    spans = [
        np.array([s[0] == piece for s in steps], np.int32) for piece in range(len(pieces))
    ]
    offsets = sum(
        jnp.stack([jnp.asarray(slot), jnp.asarray(rel), jnp.asarray(col)])[:, None].astype(jnp.int32)
        * span[None, :]
        for (_, slot, rel, col), span in zip(pieces, spans)
    )
    where = jnp.asarray(table) + offsets

    def in_map(piece):
        first = firsts[piece]
        columns = pieces[piece][0].shape[1] // tile
        count = pieces[piece][0].shape[0] // capacity * columns

        def index(step, where_ref):
            at = jnp.clip(step - first, 0, count - 1)
            return at // columns, at % columns

        return index

    return pl.pallas_call(
        functools.partial(project_kernel, firsts),
        out_shape=jax.ShapeDtypeStruct((arc_count * capacity, width), jnp.bfloat16),
        grid_spec=pltpu.PrefetchScalarGridSpec(
            num_scalar_prefetch=1,
            grid=(total,),
            in_specs=[
                pl.BlockSpec((capacity, tile), in_map(piece)) for piece in range(len(pieces))
            ]
            + [
                pl.BlockSpec((1,) + b.shape[1:], lambda s, w: (w[1, s], 0, 0))
                for b in (basis, turned)
            ],
            out_specs=pl.BlockSpec((capacity, tile), lambda s, w: (w[0, s], w[2, s])),
        ),
    )(where, *[block for block, *_ in pieces], basis, turned)


def eliminate(m_ref):
    n = m_ref.shape[0]
    blocks = n // LANES
    row = lax.broadcasted_iota(jnp.int32, (LANES, LANES), 0)
    col = lax.broadcasted_iota(jnp.int32, (LANES, LANES), 1)

    def step(i, carry):
        at = pl.ds(pl.multiple_of(i * LANES, LANES), LANES)
        inv = jnp.concatenate(inverse_factor([rows_of(m_ref[at, at])])[0], axis=0)
        m_ref[at, at] = jnp.where(row == col, 1.0, 0.0)
        m_ref[at, :] = product(inv, m_ref[at, :], ((1,), (0,)), HIGHEST)

        def update(t, carry):
            to = pl.ds(pl.multiple_of(t * LANES, LANES), LANES)
            coef = m_ref[at, to]
            m_ref[to, at] = jnp.zeros((LANES, LANES), jnp.float32)
            m_ref[to, :] = m_ref[to, :] - product(coef, m_ref[at, :], ((0,), (0,)), HIGHEST)
            return carry

        lax.fori_loop(i + 1, blocks, update, 0)
        kept = lax.broadcasted_iota(jnp.int32, (LANES, n), 1) < (i + 1) * LANES
        m_ref[at, :] = jnp.where(kept, m_ref[at, :], 0.0)
        return carry

    lax.fori_loop(0, blocks, step, 0)


def on_diagonal(values, n):
    row = lax.broadcasted_iota(jnp.int32, (n, n), 0)
    col = lax.broadcasted_iota(jnp.int32, (n, n), 1)
    return jnp.where(row == col, values, 0.0)


def first_kernel(x_ref, d_ref, m_ref):
    n = m_ref.shape[0]
    x = x_ref[...]
    m_ref[...] = product(x, x, ((0,), (0,))) + on_diagonal(d_ref[...], n)
    eliminate(m_ref)


def next_kernel(before_ref, x_ref, d_ref, prior_ref, m_ref, cross_ref):
    n = m_ref.shape[0]
    x = x_ref[...]
    cross = fine(prior_ref[...], product(before_ref[...], x, ((0,), (0,))), ((1,), (0,)))
    m_ref[...] = product(x, x, ((0,), (0,))) + on_diagonal(d_ref[...], n) - fine(
        cross, cross, ((0,), (0,))
    )
    cross_ref[...] = fine(cross, prior_ref[...], ((0,), (0,)))
    eliminate(m_ref)
    cross_ref[...] = -fine(m_ref[...], cross_ref[...], ((1,), (0,)))


def pivot_call(kernel, outs, args):
    shape = jax.ShapeDtypeStruct((PANEL, PANEL), jnp.float32)
    vmem = pl.BlockSpec(memory_space=pltpu.VMEM)
    return pl.pallas_call(
        kernel,
        out_shape=[shape] * outs,
        in_specs=[vmem] * len(args),
        out_specs=[vmem] * outs,
        compiler_params=pltpu.CompilerParams(vmem_limit_bytes=40 << 20),
    )(*args)


def per_device(plan, design, local_design, lengths, regularizer):
    row_count, col_width = design.shape
    tile_rows = regularizer.shape[0]
    own_arcs = lengths.shape[0]
    arc_count = own_arcs * plan.arc
    capacity = row_count // own_arcs
    half_arcs = own_arcs // CORES
    arc_index, trow_index = lax.axis_index("arc"), lax.axis_index("trow")
    tcol_index = lax.axis_index("tcol")
    core, x_index = tcol_index % CORES, tcol_index // CORES
    row_start = (arc_index * plan.trow + trow_index) * tile_rows
    col_start = tcol_index * col_width
    lead = PANEL * PANELS

    live_rows = jnp.arange(capacity, dtype=jnp.int32)[None, :] < lengths[:, None]
    live_flat = live_rows.reshape(row_count, 1)
    zero = jnp.zeros((), design.dtype)

    def arc_back(s):
        return lax.rem(arc_index + plan.arc - s, plan.arc)

    def pieces_of(halves, others):
        found = []
        for s in range(plan.arc):
            for block, which in ((halves[s], core), (others[s], 1 - core)):
                offset = which * half_arcs
                found.append((block, arc_back(s) * own_arcs + offset, s * own_arcs + offset, 0))
        return found

    def from_lead(arc, trow, tcol):
        return tcol < CORES

    def spread_lead(mine):
        found = []
        for s in range(plan.arc):
            arrived = [
                plan.move(mine, s, dx, from_lead) if s or dx else mine
                for dx in range(plan.across)
            ]
            best = arrived[0]
            for dx in range(1, plan.across):
                best = jnp.where(x_index == dx, arrived[dx], best)
            found.append(best)
        return found

    panel_pieces = []
    lead_sent = []
    for panel in range(PANELS):
        block = jnp.where(live_flat, design[:, panel * PANEL : (panel + 1) * PANEL], zero)
        if panel == 0:
            mine = plan.own_half(block, 0)
            halves = spread_lead(mine)
            others = jnp.split(plan.core_swap(jnp.concatenate(halves)), plan.arc)
            panel_pieces.append(pieces_of(halves, others))
        else:
            block = after(block, lead_sent[-1])
            mine = jnp.where(core == 0, block, plan.core_swap(block))
            panel_pieces.append(
                [
                    (got, arc_back(s) * own_arcs, s * own_arcs, 0)
                    for s, got in enumerate(spread_lead(mine))
                ]
            )
        lead_sent.append(mine)
    live_rows, live_flat, local_design = lax.optimization_barrier(
        (live_rows, live_flat, local_design, *lead_sent)
    )[:3]
    local_half = local_design.reshape(own_arcs, capacity, -1)
    local_half = jnp.where(live_rows[:, :, None], local_half, jnp.zeros((), local_design.dtype))

    masked = jnp.where(live_flat, design, zero)
    part = max(col_width // 2, tile_rows)
    parts = col_width // part

    def part_of(arc):
        return lax.rem((arc * plan.trow + trow_index) * tile_rows, col_width) // part

    def column_part(which):
        return lax.dynamic_slice_in_dim(masked, which * part, part, 1)

    column_pieces = [(masked, arc_index * own_arcs, 0, 0)]
    tile_parts = [masked]
    later = []
    for s in range(1, plan.arc):
        target = lax.rem(arc_index + s, plan.arc)
        for order in range(parts):
            sent = column_part(lax.rem(part_of(target) + order, parts))
            got = plan.move(sent, s, 0)
            which = lax.rem(part_of(arc_index) + order, parts)
            (column_pieces if order == 0 else later).append(
                (got, arc_back(s) * own_arcs, s * own_arcs, which)
            )
            if order == 0:
                tile_parts.append(got)

    def holder(a, r):
        return (a * plan.trow + r) * tile_rows // col_width

    my_holder = row_start // col_width

    def tile_half(s, block):
        start = lax.rem(row_start, col_width)
        if s:
            start = lax.rem(start, part)
        mine = plan.own_half(
            lax.dynamic_slice_in_dim(block, start, tile_rows, 1), my_holder % CORES
        )
        best = mine
        for dx in range(1, plan.across):
            got = plan.move(
                mine, 0, dx, lambda a, r, c: holder(a, r) // CORES == c // CORES
            )
            far = lax.rem(x_index + plan.across - my_holder // CORES, plan.across) == dx
            best = jnp.where(far, got, best)
        return mine, best

    _, own_tile = tile_half(0, masked)

    lead_tiles = -(-lead // tile_rows)
    all_regularizer = plan.gather_rows(after(regularizer, lead_sent[0]))[: lead_tiles * tile_rows][:lead]

    basis_own = local_basis(local_half)
    basis = jnp.concatenate([basis_own] + [plan.move(basis_own, s, 0) for s in range(1, plan.arc)])
    bases = (basis, jnp.transpose(basis, (0, 2, 1)))

    leads, factors = [], []
    for panel in range(PANELS):
        if panel == 1:
            bases = lax.optimization_barrier((*bases, factors[-1][-1]))[:2]
            sent = [
                tile_half(s, after(block, factors[-1][-1]))
                for s, block in enumerate(tile_parts)
                if s
            ]
        rows = project(panel_pieces[panel], bases, arc_count, PANEL)
        values = all_regularizer[None, panel * PANEL : (panel + 1) * PANEL]
        if panel == 1:
            values = after(values, *[mine for mine, _ in sent])
        if panel == 0:
            (inverse,) = pivot_call(first_kernel, 1, (rows, values))
            factors.append([inverse])
        else:
            inverse, cross = pivot_call(next_kernel, 2, (leads[0], rows, values, factors[0][0]))
            factors.append([cross, inverse])
        leads.append(rows)

    bases = lax.optimization_barrier((*bases, factors[-1][-1]))[:2]
    halves = [own_tile] + [best for _, best in sent]
    tile_pieces = pieces_of(halves, jnp.split(plan.core_swap(jnp.concatenate(halves)), plan.arc))
    tile = min(WIDTH, part)
    column_pieces = [
        (block, slot, rel, which * (part // tile)) for block, slot, rel, which in column_pieces + later
    ]
    col_rows = project(column_pieces, bases, arc_count, col_width)
    tile_cols = project(tile_pieces, bases, arc_count, tile_rows)

    rows_global = row_start + jnp.arange(tile_rows, dtype=jnp.int32)
    cols_global = col_start + jnp.arange(col_width, dtype=jnp.int32)

    def factor_of(rows, ids, panel):
        total = None
        for before in range(panel + 1):
            lead_ids = before * PANEL + jnp.arange(PANEL, dtype=jnp.int32)
            strip = product(rows, leads[before], ((0,), (0,)))
            strip = strip + jnp.where(
                ids[:, None] == lead_ids[None, :],
                all_regularizer[None, before * PANEL : (before + 1) * PANEL],
                jnp.zeros((), jnp.float32),
            )
            term = product(strip, factors[panel][before], ((1,), (1,)), lax.Precision.HIGH)
            total = term if total is None else total + term
        return jnp.where(ids[:, None] >= panel * PANEL, total, jnp.zeros((), jnp.float32))

    col_factor = [factor_of(col_rows, cols_global, panel) for panel in range(PANELS)]
    row_factor = [factor_of(tile_cols, rows_global, panel) for panel in range(PANELS)]
    normal_block = product(tile_cols, col_rows, ((0,), (0,)))
    normal_block = normal_block + jnp.where(
        rows_global[:, None] == cols_global[None, :],
        regularizer[:, None],
        jnp.zeros((), jnp.float32),
    )
    normal_block = normal_block - product(
        jnp.concatenate(row_factor, axis=1),
        jnp.concatenate(col_factor, axis=1),
        ((1,), (1,)),
        lax.Precision.HIGH,
    )
    return (normal_block, jnp.stack(col_factor))


def solution(mesh):
    plan = Plan(mesh)

    def body(*args):
        return per_device(plan, *args)

    return jax.shard_map(
        body,
        mesh=mesh,
        in_specs=(P("arc", "tcol"), P("arc", None), P("arc"), P(("arc", "trow"))),
        out_specs=(P(("arc", "trow"), "tcol"), P(None, "tcol", None)),
        check_vma=False,
    )
```

```python
import functools

import jax
import jax.numpy as jnp
from jax import lax
from jax.experimental import pallas as pl
from jax.experimental.pallas import tpu as pltpu
from jax.sharding import PartitionSpec as P

PANEL = 512
PANELS = 2
AXES = ("arc", "trow", "tcol")
CORES = 2


ridge = 0.1

HIGHEST = lax.Precision.HIGHEST
LANES = 128
CHUNK = 256
SUB = 8


def inverse_factor(rows_list):
    groups = LANES // SUB
    lane = lax.broadcasted_iota(jnp.int32, (SUB, LANES), 1)
    sub = lax.broadcasted_iota(jnp.int32, (SUB, LANES), 0)
    outs = [[] for _ in rows_list]
    state = [list(rows) for rows in rows_list]
    for s in range(groups):
        j = s * SUB
        inside = (lane >= j) & (lane < j + SUB)
        for b, rows in enumerate(state):
            lead = rows[s]
            unit = jnp.where(lane == sub + j, 1.0, 0.0)
            merged = jnp.where(inside, unit, lead)
            z = [jnp.broadcast_to(merged[k:k + 1, :], (SUB, LANES)) for k in range(SUB)]
            sp = {
                (m, k): jnp.broadcast_to(lead[k:k + 1, j + m:j + m + 1], (SUB, LANES))
                for k in range(SUB) for m in range(k, SUB)
            }
            below = list(range(s + 1, groups))
            col = {
                (t, k): jnp.broadcast_to(rows[t][:, j + k:j + k + 1], (SUB, LANES))
                for t in below for k in range(SUB)
            }
            rest = {t: jnp.where(inside, 0.0, rows[t]) for t in below}
            for k in range(SUB):
                inv = lax.rsqrt(sp[k, k])
                z[k] = z[k] * inv
                l = {m: sp[m, k] * inv for m in range(k + 1, SUB)}
                for m in range(k + 1, SUB):
                    for n in range(m, SUB):
                        sp[n, m] = sp[n, m] - l[n] * l[m]
                for m in range(k + 1, SUB):
                    z[m] = z[m] - l[m] * z[k]
                for t in below:
                    c = col[t, k] * inv
                    for m in range(k + 1, SUB):
                        col[t, m] = col[t, m] - c * l[m]
                    rest[t] = rest[t] - c * z[k]
            for t in below:
                rows[t] = rest[t]
            done = z[0]
            for k in range(1, SUB):
                done = jnp.where(sub == k, z[k], done)
            outs[b].append(jnp.where(lane <= sub + j, done, 0.0))
    return outs


def rows_of(block):
    return [block[SUB * t:SUB * (t + 1), :] for t in range(LANES // SUB)]


class Plan:
    def __init__(self, mesh):
        self.arc, self.trow, self.tcol = (mesh.shape[name] for name in AXES)
        self.across = self.tcol // CORES

    def flat(self, arc, trow, tcol):
        return (arc % self.arc * self.trow + trow) * self.tcol + tcol % self.tcol

    def move(self, block, arcs, across, source=None):
        pairs = [
            (self.flat(a, r, c), self.flat(a + arcs, r, c + across * CORES))
            for a in range(self.arc)
            for r in range(self.trow)
            for c in range(self.tcol)
            if source is None or source(a, r, c)
        ]
        return lax.ppermute(block, AXES, pairs)

    def core_swap(self, block):
        pairs = [
            (self.flat(a, r, c), self.flat(a, r, c ^ 1))
            for a in range(self.arc)
            for r in range(self.trow)
            for c in range(self.tcol)
        ]
        return lax.ppermute(block, AXES, pairs)

    def own_half(self, block, holder_core):
        half = block.shape[0] // CORES
        core = lax.axis_index("tcol") % CORES
        got = self.core_swap(block)
        mine = lax.dynamic_slice_in_dim(block, core * half, half, 0)
        theirs = lax.dynamic_slice_in_dim(got, core * half, half, 0)
        return jnp.where(core == holder_core, mine, theirs)

    def gather_rows(self, tile):
        me = lax.axis_index("arc") * self.trow + lax.axis_index("trow")
        total = self.arc * self.trow
        spans = [self.trow << n for n in range(self.arc.bit_length() - 1)]
        spans += [1 << n for n in range(self.trow.bit_length() - 1)]
        tile = tile[None]
        for span in spans:
            pairs = [
                (t * self.tcol + c, (t ^ span) * self.tcol + c)
                for t in range(total)
                for c in range(self.tcol)
            ]
            got = lax.ppermute(tile, AXES, pairs)
            low = (me & span) == 0
            tile = jnp.concatenate([jnp.where(low, tile, got), jnp.where(low, got, tile)])
        blocks = tile.reshape(self.trow, self.arc, -1)
        return jnp.transpose(blocks, (1, 0, 2)).reshape(-1)


def local_kernel(a_ref, n_ref):
    count = a_ref.shape[0]
    found = inverse_factor([rows_of(a_ref[b]) for b in range(count)])
    for b in range(count):
        n_ref[b] = jnp.concatenate(found[b], axis=0)


def local_call(a):
    return pl.pallas_call(
        local_kernel,
        out_shape=jax.ShapeDtypeStruct(a.shape, jnp.float32),
        in_specs=[pl.BlockSpec(memory_space=pltpu.VMEM)],
        out_specs=pl.BlockSpec(memory_space=pltpu.VMEM),
        name="local_inverse",
    )(a)


def local_basis(local_half):
    local_normal = jnp.einsum(
        "acl,acm->alm", local_half, local_half, preferred_element_type=jnp.float32
    )
    local_normal = local_normal + ridge * jnp.eye(local_half.shape[2], dtype=jnp.float32)[None]
    inverse = local_call(local_normal)
    basis_rows = jnp.einsum(
        "alm,acm->alc", inverse, local_half.astype(jnp.float32), precision=HIGHEST
    )
    return basis_rows.astype(jnp.bfloat16)


def after(value, *earlier):
    return lax.optimization_barrier((value,) + earlier)[0]


def product(left, right, dims, precision=None):
    return lax.dot_general(
        left, right, (dims, ((), ())), precision=precision, preferred_element_type=jnp.float32
    )


def fine(left, right, dims):
    left_top, right_top = left.astype(jnp.bfloat16), right.astype(jnp.bfloat16)
    left_rest = (left - left_top.astype(jnp.float32)).astype(jnp.bfloat16)
    right_rest = (right - right_top.astype(jnp.float32)).astype(jnp.bfloat16)
    return product(left_top, right_top, dims) + (
        product(left_top, right_rest, dims) + product(left_rest, right_top, dims)
    )


def eliminate(m_ref):
    n = m_ref.shape[0]
    blocks = n // LANES
    row = lax.broadcasted_iota(jnp.int32, (LANES, LANES), 0)
    col = lax.broadcasted_iota(jnp.int32, (LANES, LANES), 1)

    def step(i, carry):
        at = pl.ds(pl.multiple_of(i * LANES, LANES), LANES)
        inv = jnp.concatenate(inverse_factor([rows_of(m_ref[at, at])])[0], axis=0)
        m_ref[at, at] = jnp.where(row == col, 1.0, 0.0)
        m_ref[at, :] = product(inv, m_ref[at, :], ((1,), (0,)), HIGHEST)

        def update(t, carry):
            to = pl.ds(pl.multiple_of(t * LANES, LANES), LANES)
            coef = m_ref[at, to]
            m_ref[to, at] = jnp.zeros((LANES, LANES), jnp.float32)
            m_ref[to, :] = m_ref[to, :] - product(coef, m_ref[at, :], ((0,), (0,)), HIGHEST)
            return carry

        lax.fori_loop(i + 1, blocks, update, 0)
        kept = lax.broadcasted_iota(jnp.int32, (LANES, n), 1) < (i + 1) * LANES
        m_ref[at, :] = jnp.where(kept, m_ref[at, :], 0.0)
        return carry

    lax.fori_loop(0, blocks, step, 0)


def on_diagonal(values, n):
    row = lax.broadcasted_iota(jnp.int32, (n, n), 0)
    col = lax.broadcasted_iota(jnp.int32, (n, n), 1)
    return jnp.where(row == col, values, 0.0)


def clean(block, basis, turned):
    loadings = product(basis, block, ((1,), (0,))).astype(jnp.bfloat16)
    return (block.astype(jnp.float32) - product(turned, loadings, ((1,), (0,)))).astype(
        jnp.bfloat16
    )


def clean_pieces(choices, layout, table_ref, base, basis_ref, turned_ref, out_ref):
    capacity = basis_ref.shape[2]
    for n, (candidates, at) in enumerate(layout):
        slot, rel, chosen = (table_ref[base + 3 * n + i] for i in range(3))
        to = pl.ds(pl.multiple_of(slot * capacity, 64), capacity)
        rows = slice(at * capacity, (at + 1) * capacity)

        def put(ref, to=to, rows=rows, rel=rel):
            out_ref[to, :] = clean(ref[rows, :], basis_ref[rel], turned_ref[rel])

        if len(candidates) == 1:
            put(choices[candidates[0]])
            continue
        for which, candidate in enumerate(candidates):

            @pl.when(chosen == which)
            def _(put=put, candidate=candidate):
                put(choices[candidate])


def turn_bases(basis_ref, turned_ref):
    for a in range(basis_ref.shape[0]):
        turned_ref[a] = basis_ref[a].T


def split(value):
    top = value.astype(jnp.bfloat16)
    return top, (value - top.astype(jnp.float32)).astype(jnp.bfloat16)


def first_kernel(pieces, layout, table_ref, d_ref, basis_ref, *refs):
    piece_refs = refs[:pieces]
    x_ref, m_ref, top_ref, rest_ref, md_ref, turned_ref = refs[pieces:]
    turn_bases(basis_ref, turned_ref)
    n = m_ref.shape[0]
    clean_pieces(piece_refs, layout, table_ref, 0, basis_ref, turned_ref, x_ref)
    x = x_ref[...]
    m_ref[...] = product(x, x, ((0,), (0,))) + on_diagonal(d_ref[...], n)
    eliminate(m_ref)
    inverse = m_ref[...]
    inv_top, inv_rest = split(inverse)
    x = x_ref[...]
    top_ref[...], rest_ref[...] = split(
        product(x, inv_top, ((1,), (1,))) + product(x, inv_rest, ((1,), (1,)))
    )
    md_ref[...] = (inverse * d_ref[...]).T


def next_kernel(pieces, layout, table_ref, d_ref, basis_ref, *refs):
    piece_refs = refs[:pieces]
    before_ref, prior_ref, top_ref, rest_ref, md_ref, turned_ref, x_ref, m_ref, cross_ref = refs[
        pieces:
    ]
    turn_bases(basis_ref, turned_ref)
    n = m_ref.shape[0]
    clean_pieces(piece_refs, layout, table_ref, 0, basis_ref, turned_ref, x_ref)
    x = x_ref[...]
    cross = fine(prior_ref[...], product(before_ref[...], x, ((0,), (0,))), ((1,), (0,)))
    m_ref[...] = product(x, x, ((0,), (0,))) + on_diagonal(d_ref[...], n) - fine(
        cross, cross, ((0,), (0,))
    )
    cross_ref[...] = fine(cross, prior_ref[...], ((0,), (0,)))
    eliminate(m_ref)
    inverse = m_ref[...]
    back = -fine(inverse, cross_ref[...], ((1,), (0,)))
    total = None
    for rows, factor in ((x_ref, inverse), (before_ref, back)):
        top, rest = split(factor)
        rows = rows[...]
        term = product(rows, top, ((1,), (1,))) + product(rows, rest, ((1,), (1,)))
        total = term if total is None else total + term
    top_ref[...], rest_ref[...] = split(total)
    md_ref[...] = (inverse * d_ref[...]).T


def pivot_call(panel, layout, table, values, basis, pieces, prior):
    rows = basis.shape[0] * basis.shape[2]
    square = jax.ShapeDtypeStruct((PANEL, PANEL), jnp.float32)
    tall = jax.ShapeDtypeStruct((rows, PANEL), jnp.bfloat16)
    vmem = pl.BlockSpec(memory_space=pltpu.VMEM)
    kernel, outs, scratch, _ = (
        (first_kernel, [tall, square, tall, tall, square], [], "pivot_first")
        if panel == 0
        else (
            next_kernel,
            [tall, tall, square],
            [
                pltpu.VMEM((rows, PANEL), jnp.bfloat16),
                pltpu.VMEM((PANEL, PANEL), jnp.float32),
                pltpu.VMEM((PANEL, PANEL), jnp.float32),
            ],
            "pivot_next",
        )
    )
    scratch = [pltpu.VMEM((basis.shape[0], *basis.shape[:0:-1]), jnp.bfloat16)] + scratch
    args = (values[None, :], basis, *pieces, *prior)
    return pl.pallas_call(
        functools.partial(kernel, len(pieces), layout),
        out_shape=outs,
        in_specs=[pl.BlockSpec(memory_space=pltpu.SMEM)] + [vmem] * len(args),
        out_specs=[vmem] * len(outs),
        scratch_shapes=scratch,
        compiler_params=pltpu.CompilerParams(vmem_limit_bytes=56 << 20),
    )(table, *args)


def assemble_kernel(spec, table_ref, own_ref, *refs):
    arcs, own_arcs, pieces, layout = spec
    got_refs, refs = refs[: arcs - 1], refs[arcs - 1 :]
    tile_refs, refs = refs[:pieces], refs[pieces:]
    basis_ref, top0, top1, rest0, rest1, md0, md1, d_ref = refs[:8]
    normal_ref, panel_ref, turned_ref, xc, xct, xr, xrt, fr_top, fr_rest, fc_top, fc_rest, work = (
        refs[8:]
    )
    width, tile_rows = xc.shape[1], xr.shape[1]
    total_rows = xc.shape[0]
    row_start = table_ref[0]
    tile_start = table_ref[1] + pl.program_id(0) * width
    chunk = min(CHUNK, tile_rows, width)

    def turn(source, target):
        for at in range(0, total_rows, LANES):
            target[:, at : at + LANES] = source[at : at + LANES, :].T

    def factor(xt_ref, at, start):
        xt = xt_ref[at, :]
        for panel, (top, rest) in enumerate(((top0, rest0), (top1, rest1))):
            to = slice(panel * PANEL, (panel + 1) * PANEL)
            work[:, to] = product(xt, top[...], ((1,), (0,))) + product(xt, rest[...], ((1,), (0,)))
        for panel, md in enumerate((md0, md1)):
            to = slice(panel * PANEL, (panel + 1) * PANEL)

            @pl.when((start >= panel * PANEL) & (start < (panel + 1) * PANEL))
            def _(to=to, md=md, panel=panel):
                off = pl.multiple_of(start - panel * PANEL, chunk)
                work[:, to] = work[:, to] + md[pl.ds(off, chunk), :]

            @pl.when(start < panel * PANEL)
            def _(to=to):
                work[:, to] = jnp.zeros((chunk, PANEL), jnp.float32)

    @pl.when(pl.program_id(0) == 0)
    def _():
        turn_bases(basis_ref, turned_ref)
        clean_pieces(tile_refs, layout, table_ref, 2, basis_ref, turned_ref, xr)
        turn(xr, xrt)

        def row_chunk(i, carry):
            at = pl.ds(pl.multiple_of(i * chunk, chunk), chunk)
            factor(xrt, at, row_start + i * chunk)
            fr_top[at, :], fr_rest[at, :] = split(work[...])
            return carry

        lax.fori_loop(0, tile_rows // chunk, row_chunk, 0)

    columns = [((s,), a) for s in range(arcs) for a in range(own_arcs)]
    clean_pieces(
        [own_ref, *got_refs], columns, table_ref, 2 + 3 * len(layout), basis_ref, turned_ref, xc
    )
    turn(xc, xct)

    def col_chunk(i, carry):
        at = pl.ds(pl.multiple_of(i * chunk, chunk), chunk)
        factor(xct, at, tile_start + i * chunk)
        for panel in range(PANELS):
            panel_ref[panel, at, :] = work[:, panel * PANEL : (panel + 1) * PANEL]
        fc_top[at, :], fc_rest[at, :] = split(work[...])
        return carry

    lax.fori_loop(0, width // chunk, col_chunk, 0)
    d = d_ref[:, pl.ds(pl.multiple_of(jnp.clip(tile_start - row_start, 0, tile_rows - width), LANES), width)]

    def normal_chunk(i, carry):
        at = pl.ds(pl.multiple_of(i * chunk, chunk), chunk)
        dims = ((1,), (1,))
        value = product(xrt[at, :], xc[...], ((1,), (0,))) - (
            product(fr_top[at, :], fc_top[...], dims)
            + (product(fr_top[at, :], fc_rest[...], dims) + product(fr_rest[at, :], fc_top[...], dims))
        )
        row = lax.broadcasted_iota(jnp.int32, (chunk, width), 0) + (row_start + i * chunk)
        col = lax.broadcasted_iota(jnp.int32, (chunk, width), 1) + tile_start
        normal_ref[at, :] = value + jnp.where(row == col, d, 0.0)
        return carry

    lax.fori_loop(0, tile_rows // chunk, normal_chunk, 0)


def assemble(own, got, tiles, layout, basis, tops, rests, mds, regularizer, table, own_arcs):
    arcs = len(got) + 1
    rows = own.shape[0] * arcs
    col_width, tile_rows = own.shape[1], regularizer.shape[0]
    width = min(512 if rows <= 2048 else 256, col_width, tile_rows)
    depth = PANEL * PANELS
    chunk = min(CHUNK, tile_rows, width)
    once = pl.Buffered(1)

    def whole(array):
        zeros = (0,) * array.ndim
        return pl.BlockSpec(array.shape, lambda s, t: zeros, pipeline_mode=once)

    fixed = [*tiles, basis, *tops, *rests, *mds, regularizer[None, :]]
    columns = pl.BlockSpec((own.shape[0], width), lambda s, t: (0, s))
    return pl.pallas_call(
        functools.partial(assemble_kernel, (arcs, own_arcs, len(tiles), layout)),
        out_shape=(
            jax.ShapeDtypeStruct((tile_rows, col_width), jnp.float32),
            jax.ShapeDtypeStruct((PANELS, col_width, PANEL), jnp.float32),
        ),
        grid_spec=pltpu.PrefetchScalarGridSpec(
            num_scalar_prefetch=1,
            grid=(col_width // width,),
            in_specs=[columns] * arcs + [whole(array) for array in fixed],
            out_specs=(
                pl.BlockSpec((tile_rows, width), lambda s, t: (0, s)),
                pl.BlockSpec((PANELS, width, PANEL), lambda s, t: (0, s, 0)),
            ),
            scratch_shapes=[
                pltpu.VMEM((basis.shape[0], *basis.shape[:0:-1]), jnp.bfloat16),
                pltpu.VMEM((rows, width), jnp.bfloat16),
                pltpu.VMEM((width, rows), jnp.bfloat16),
                pltpu.VMEM((rows, tile_rows), jnp.bfloat16),
                pltpu.VMEM((tile_rows, rows), jnp.bfloat16),
                pltpu.VMEM((tile_rows, depth), jnp.bfloat16),
                pltpu.VMEM((tile_rows, depth), jnp.bfloat16),
                pltpu.VMEM((width, depth), jnp.bfloat16),
                pltpu.VMEM((width, depth), jnp.bfloat16),
                pltpu.VMEM((chunk, depth), jnp.float32),
            ],
        ),
        compiler_params=pltpu.CompilerParams(vmem_limit_bytes=60 << 20),
        name="assemble",
    )(table, own, *got, *fixed)


def per_device(plan, design, local_design, lengths, regularizer):
    row_count, col_width = design.shape
    tile_rows = regularizer.shape[0]
    own_arcs = lengths.shape[0]
    capacity = row_count // own_arcs
    half_arcs = own_arcs // CORES
    arc_index, trow_index = lax.axis_index("arc"), lax.axis_index("trow")
    tcol_index = lax.axis_index("tcol")
    core, x_index = tcol_index % CORES, tcol_index // CORES
    row_start = (arc_index * plan.trow + trow_index) * tile_rows
    col_start = tcol_index * col_width
    lead = PANEL * PANELS

    live_rows = jnp.arange(capacity, dtype=jnp.int32)[None, :] < lengths[:, None]
    live_flat = live_rows.reshape(row_count, 1)
    zero = jnp.zeros((), design.dtype)

    def arc_back(s):
        return lax.rem(arc_index + plan.arc - s, plan.arc)

    def half_entries(halves_count):
        layout, entries = [], []
        for n, which in enumerate((core, 1 - core)):
            for s in range(plan.arc):
                for a in range(half_arcs):
                    offset = which * half_arcs + a
                    layout.append(((n * halves_count + s,), a))
                    entries += [arc_back(s) * own_arcs + offset, s * own_arcs + offset, 0]
        return layout, entries

    def from_lead(arc, trow, tcol):
        return tcol < CORES

    def spread_lead(mine):
        return [
            [plan.move(mine, s, dx, from_lead) if s or dx else mine for dx in range(plan.across)]
            for s in range(plan.arc)
        ]

    def lead_block(panel, live):
        return jnp.where(live, design[:, panel * PANEL : (panel + 1) * PANEL], zero)

    mine = plan.own_half(lead_block(0, live_flat), 0)
    halves = []
    for arrived in spread_lead(mine):
        best = arrived[0]
        for dx in range(1, plan.across):
            best = jnp.where(x_index == dx, arrived[dx], best)
        halves.append(best)
    first_pieces = halves + [plan.core_swap(half) for half in halves]

    live_rows, local_design, regularizer_sent = lax.optimization_barrier(
        (live_rows, local_design, regularizer, mine)
    )[:3]
    local_half = local_design.reshape(own_arcs, capacity, -1)
    local_half = jnp.where(live_rows[:, :, None], local_half, jnp.zeros((), local_design.dtype))
    basis_own = local_basis(local_half)
    basis = jnp.concatenate([basis_own] + [plan.move(basis_own, s, 0) for s in range(1, plan.arc)])

    live_flat = after(live_flat, basis_own)
    block = lead_block(1, live_flat)
    mine = jnp.where(core == 0, block, plan.core_swap(block))
    arrivals = spread_lead(mine)
    next_pieces = [got for arrived in arrivals for got in arrived]
    next_layout = [
        (tuple(s * plan.across + dx for dx in range(plan.across)), a)
        for s in range(plan.arc)
        for a in range(own_arcs)
    ]
    live_flat = after(live_flat, mine)

    masked = jnp.where(live_flat, design, zero)
    got_columns = [plan.move(masked, s, 0) for s in range(1, plan.arc)]

    def holder(a, r):
        return (a % plan.arc * plan.trow + r) * tile_rows // col_width

    my_holder = row_start // col_width
    halves = []
    for s in range(plan.arc):
        target = (lax.rem(arc_index + s, plan.arc) * plan.trow + trow_index) * tile_rows
        tile = lax.dynamic_slice_in_dim(masked, lax.rem(target, col_width), tile_rows, 1)
        mine = plan.own_half(tile, target // col_width % CORES)

        def has_tile(a, r, c, s=s):
            return holder(a + s, r) // CORES == c // CORES

        arrived = [
            plan.move(mine, s, dx, has_tile) if s or dx else mine
            for dx in range(plan.across)
        ]
        best = arrived[0]
        for dx in range(1, plan.across):
            far = lax.rem(x_index + plan.across - my_holder // CORES, plan.across) == dx
            best = jnp.where(far, arrived[dx], best)
        halves.append(best)

    lead_tiles = -(-lead // tile_rows)
    all_regularizer = plan.gather_rows(regularizer_sent)[: lead_tiles * tile_rows][:lead]

    def table_of(*values):
        return jnp.stack([jnp.asarray(v, jnp.int32) for v in values])

    layout, entries = half_entries(plan.arc)
    first_rows, prior, *first_parts = pivot_call(
        0, layout, table_of(*entries), all_regularizer[:PANEL], basis, first_pieces, ()
    )

    def arc_entries(chosen):
        return [
            v
            for s in range(plan.arc)
            for a in range(own_arcs)
            for v in (arc_back(s) * own_arcs + a, s * own_arcs + a, chosen)
        ]

    next_parts = pivot_call(
        1,
        next_layout,
        table_of(*arc_entries(x_index)),
        all_regularizer[PANEL:lead],
        basis,
        next_pieces,
        (first_rows, prior),
    )
    tiles = halves + [plan.core_swap(half) for half in halves]
    return assemble(
        masked,
        got_columns,
        tiles,
        layout,
        basis,
        *[[a, b] for a, b in zip(first_parts, next_parts)],
        regularizer,
        table_of(row_start, col_start, *entries, *arc_entries(0)),
        own_arcs,
    )


def solution(mesh):
    plan = Plan(mesh)

    def body(*args):
        return per_device(plan, *args)

    return jax.shard_map(
        body,
        mesh=mesh,
        in_specs=(P("arc", "tcol"), P("arc", None), P("arc"), P(("arc", "trow"))),
        out_specs=(P(("arc", "trow"), "tcol"), P(None, "tcol", None)),
        check_vma=False,
    )
```

```python
import functools

import jax
import jax.numpy as jnp
from jax import lax
from jax.experimental import pallas as pl
from jax.experimental.pallas import tpu as pltpu
from jax.sharding import PartitionSpec as P

PANEL = 512
PANELS = 2
AXES = ("arc", "trow", "tcol")
CORES = 2


ridge = 0.1

HIGHEST = lax.Precision.HIGHEST
LANES = 128
CHUNK = 512
SUB = 8


def inverse_factor(rows):
    groups = LANES // SUB
    rows = list(rows)
    lane = lax.broadcasted_iota(jnp.int32, (SUB, LANES), 1)
    sub = lax.broadcasted_iota(jnp.int32, (SUB, LANES), 0)
    shape = (SUB, LANES)
    out = []
    for s in range(groups):
        j = s * SUB
        inside = (lane >= j) & (lane < j + SUB)
        lead = rows[s]
        merged = jnp.where(inside, jnp.where(lane == sub + j, 1.0, 0.0), lead)
        z = [jnp.broadcast_to(merged[k : k + 1, :], shape) for k in range(SUB)]
        sp = {
            (m, k): jnp.broadcast_to(lead[k : k + 1, j + m : j + m + 1], shape)
            for k in range(SUB)
            for m in range(k, SUB)
        }
        below = range(s + 1, groups)
        col = {
            (t, k): jnp.broadcast_to(rows[t][:, j + k : j + k + 1], shape)
            for t in below
            for k in range(SUB)
        }
        rest = {t: jnp.where(inside, 0.0, rows[t]) for t in below}
        for k in range(0, SUB, 2):
            a, b, c = sp[k, k], sp[k + 1, k], sp[k + 1, k + 1]
            det = a * c - b * b
            root = lax.rsqrt(det)
            scale = root * root
            pair = {
                m: (c * sp[m, k] - b * sp[m, k + 1], a * sp[m, k + 1] - b * sp[m, k])
                for m in range(k + 2, SUB)
            }
            first = lax.rsqrt(a)
            second = root * (a * first)
            one = {m: sp[m, k] * first for m in range(k + 1, SUB)}
            two = {m: (sp[m, k + 1] - one[k + 1] * one[m]) * second for m in range(k + 2, SUB)}
            for m in range(k + 2, SUB):
                for n in range(m, SUB):
                    sp[n, m] = sp[n, m] - (sp[n, k] * pair[m][0] + sp[n, k + 1] * pair[m][1]) * scale
            for at, inv, l in ((k, first, one), (k + 1, second, two)):
                z[at] = z[at] * inv
                for m in range(at + 1, SUB):
                    z[m] = z[m] - l[m] * z[at]
                for t in below:
                    coef = col[t, at] * inv
                    for m in range(at + 1, SUB):
                        col[t, m] = col[t, m] - coef * l[m]
                    rest[t] = rest[t] - coef * z[at]
        for t in below:
            rows[t] = rest[t]
        done = z[0]
        for k in range(1, SUB):
            done = jnp.where(sub == k, z[k], done)
        out.append(jnp.where(lane <= sub + j, done, 0.0))
    return out


def rows_of(block):
    return [block[SUB * t:SUB * (t + 1), :] for t in range(LANES // SUB)]


class Plan:
    def __init__(self, mesh):
        self.arc, self.trow, self.tcol = (mesh.shape[name] for name in AXES)
        self.across = self.tcol // CORES

    def flat(self, arc, trow, tcol):
        return (arc % self.arc * self.trow + trow) * self.tcol + tcol % self.tcol

    def move(self, block, arcs, across, source=None):
        pairs = [
            (self.flat(a, r, c), self.flat(a + arcs, r, c + across * CORES))
            for a in range(self.arc)
            for r in range(self.trow)
            for c in range(self.tcol)
            if source is None or source(a, r, c)
        ]
        return lax.ppermute(block, AXES, pairs)

    def core_swap(self, block):
        pairs = [
            (self.flat(a, r, c), self.flat(a, r, c ^ 1))
            for a in range(self.arc)
            for r in range(self.trow)
            for c in range(self.tcol)
        ]
        return lax.ppermute(block, AXES, pairs)

    def own_half(self, block, holder_core):
        half = block.shape[0] // CORES
        core = lax.axis_index("tcol") % CORES
        got = self.core_swap(block)
        mine = lax.dynamic_slice_in_dim(block, core * half, half, 0)
        theirs = lax.dynamic_slice_in_dim(got, core * half, half, 0)
        return jnp.where(core == holder_core, mine, theirs)

    def gather_rows(self, tile):
        me = lax.axis_index("arc") * self.trow + lax.axis_index("trow")
        total = self.arc * self.trow
        spans = [self.trow << n for n in range(self.arc.bit_length() - 1)]
        spans += [1 << n for n in range(self.trow.bit_length() - 1)]
        tile = tile[None]
        for span in spans:
            pairs = [
                (t * self.tcol + c, (t ^ span) * self.tcol + c)
                for t in range(total)
                for c in range(self.tcol)
            ]
            got = lax.ppermute(tile, AXES, pairs)
            low = (me & span) == 0
            tile = jnp.concatenate([jnp.where(low, tile, got), jnp.where(low, got, tile)])
        blocks = tile.reshape(self.trow, self.arc, -1)
        return jnp.transpose(blocks, (1, 0, 2)).reshape(-1)


def local_kernel(a_ref, n_ref):
    n_ref[0] = jnp.concatenate(inverse_factor(rows_of(a_ref[0])), axis=0)


def local_call(a):
    block = pl.BlockSpec((1,) + a.shape[1:], lambda i: (i, 0, 0))
    return pl.pallas_call(
        local_kernel,
        out_shape=jax.ShapeDtypeStruct(a.shape, jnp.float32),
        grid=(a.shape[0],),
        in_specs=[block],
        out_specs=block,
        name="local_inverse",
    )(a)


def local_basis(local_half):
    local_normal = jnp.einsum(
        "acl,acm->alm", local_half, local_half, preferred_element_type=jnp.float32
    )
    local_normal = local_normal + ridge * jnp.eye(local_half.shape[2], dtype=jnp.float32)[None]
    inverse = local_call(local_normal)
    basis_rows = jnp.einsum(
        "alm,acm->alc", inverse, local_half.astype(jnp.float32), precision=HIGHEST
    )
    return basis_rows.astype(jnp.bfloat16)


def after(value, *earlier):
    return lax.optimization_barrier((value,) + earlier)[0]


def product(left, right, dims, precision=None):
    return lax.dot_general(
        left, right, (dims, ((), ())), precision=precision, preferred_element_type=jnp.float32
    )


def fine(left, right, dims):
    left_top, right_top = left.astype(jnp.bfloat16), right.astype(jnp.bfloat16)
    left_rest = (left - left_top.astype(jnp.float32)).astype(jnp.bfloat16)
    right_rest = (right - right_top.astype(jnp.float32)).astype(jnp.bfloat16)
    return product(left_top, right_top, dims) + (
        product(left_top, right_rest, dims) + product(left_rest, right_top, dims)
    )


def eliminate(m_ref):
    n = m_ref.shape[0]
    blocks = n // LANES
    row = lax.broadcasted_iota(jnp.int32, (LANES, LANES), 0)
    col = lax.broadcasted_iota(jnp.int32, (LANES, LANES), 1)

    def step(i, carry):
        at = pl.ds(pl.multiple_of(i * LANES, LANES), LANES)
        inv = jnp.concatenate(inverse_factor(rows_of(m_ref[at, at])), axis=0)
        m_ref[at, at] = jnp.where(row == col, 1.0, 0.0)
        m_ref[at, :] = fine(inv, m_ref[at, :], ((1,), (0,)))

        def update(t, carry):
            to = pl.ds(pl.multiple_of(t * LANES, LANES), LANES)
            coef = m_ref[at, to]
            m_ref[to, at] = jnp.zeros((LANES, LANES), jnp.float32)
            m_ref[to, :] = m_ref[to, :] - fine(coef, m_ref[at, :], ((0,), (0,)))
            return carry

        lax.fori_loop(i + 1, blocks, update, 0)
        kept = lax.broadcasted_iota(jnp.int32, (LANES, n), 1) < (i + 1) * LANES
        m_ref[at, :] = jnp.where(kept, m_ref[at, :], 0.0)
        return carry

    lax.fori_loop(0, blocks, step, 0)


def on_diagonal(values, n):
    row = lax.broadcasted_iota(jnp.int32, (n, n), 0)
    col = lax.broadcasted_iota(jnp.int32, (n, n), 1)
    return jnp.where(row == col, values, 0.0)


def clean(block, basis, turned):
    loadings = product(basis, block, ((1,), (0,))).astype(jnp.bfloat16)
    return (block.astype(jnp.float32) - product(turned, loadings, ((1,), (0,)))).astype(
        jnp.bfloat16
    )


def clean_pieces(choices, layout, table_ref, base, basis_ref, turned_ref, out_ref):
    capacity = basis_ref.shape[2]
    for n, (candidates, at) in enumerate(layout):
        slot, rel, chosen = (table_ref[base + 3 * n + i] for i in range(3))
        to = pl.ds(pl.multiple_of(slot * capacity, 64), capacity)
        rows = slice(at * capacity, (at + 1) * capacity)

        def put(ref, to=to, rows=rows, rel=rel):
            out_ref[to, :] = clean(ref[rows, :], basis_ref[rel], turned_ref[rel])

        if len(candidates) == 1:
            put(choices[candidates[0]])
            continue
        for which, candidate in enumerate(candidates):

            @pl.when(chosen == which)
            def _(put=put, candidate=candidate):
                put(choices[candidate])


def turn_bases(moved_refs, basis_ref, turned_ref):
    for s, moved in enumerate(moved_refs):
        for a in range(moved.shape[0]):
            basis_ref[s * moved.shape[0] + a] = moved[a]
            turned_ref[s * moved.shape[0] + a] = moved[a].T


def split(value):
    top = value.astype(jnp.bfloat16)
    return top, (value - top.astype(jnp.float32)).astype(jnp.bfloat16)


def weigh(terms, top_ref, rest_ref):
    rows = top_ref.shape[0]
    chunk = next(n for n in (512, 320, 256, LANES, SUB) if rows % n == 0 and rows > n)
    parts = [(ref, *split(factor)) for ref, factor in terms]

    def step(i, carry):
        at = pl.ds(pl.multiple_of(i * chunk, chunk), chunk)
        total = None
        for ref, top, rest in parts:
            x = ref[at, :]
            term = product(x, top, ((1,), (1,))) + product(x, rest, ((1,), (1,)))
            total = term if total is None else total + term
        top_ref[at, :], rest_ref[at, :] = split(total)
        return carry

    lax.fori_loop(0, rows // chunk, step, 0)


def first_kernel(arcs, pieces, layout, table_ref, d_ref, *refs):
    moved, refs = refs[:arcs], refs[arcs:]
    piece_refs = refs[:pieces]
    x_ref, m_ref, top_ref, rest_ref, md_ref, basis_ref, turned_ref = refs[pieces:]
    turn_bases(moved, basis_ref, turned_ref)
    n = m_ref.shape[0]
    clean_pieces(piece_refs, layout, table_ref, 0, basis_ref, turned_ref, x_ref)
    x = x_ref[...]
    m_ref[...] = product(x, x, ((0,), (0,))) + on_diagonal(d_ref[...], n)
    eliminate(m_ref)
    inverse = m_ref[...]
    weigh([(x_ref, inverse)], top_ref, rest_ref)
    md_ref[...] = (inverse * d_ref[...]).T


def next_kernel(arcs, pieces, layout, table_ref, d_ref, *refs):
    moved, refs = refs[:arcs], refs[arcs:]
    piece_refs, refs = refs[:pieces], refs[pieces:]
    before_ref, prior_ref, top_ref, rest_ref, md_ref = refs[:5]
    basis_ref, turned_ref, x_ref, m_ref, cross_ref = refs[5:]
    turn_bases(moved, basis_ref, turned_ref)
    n = m_ref.shape[0]
    clean_pieces(piece_refs, layout, table_ref, 0, basis_ref, turned_ref, x_ref)
    x = x_ref[...]
    cross = fine(prior_ref[...], product(before_ref[...], x, ((0,), (0,))), ((1,), (0,)))
    m_ref[...] = product(x, x, ((0,), (0,))) + on_diagonal(d_ref[...], n) - fine(
        cross, cross, ((0,), (0,))
    )
    cross_ref[...] = fine(cross, prior_ref[...], ((0,), (0,)))
    eliminate(m_ref)
    inverse = m_ref[...]
    back = -fine(inverse, cross_ref[...], ((1,), (0,)))
    weigh([(x_ref, inverse), (before_ref, back)], top_ref, rest_ref)
    md_ref[...] = (inverse * d_ref[...]).T


def pivot_call(panel, layout, table, values, basis, pieces, prior):
    own_arcs, local, capacity = basis[0].shape
    rows = own_arcs * len(basis) * capacity
    square = jax.ShapeDtypeStruct((PANEL, PANEL), jnp.float32)
    tall = jax.ShapeDtypeStruct((rows, PANEL), jnp.bfloat16)
    vmem = pl.BlockSpec(memory_space=pltpu.VMEM)
    kernel, outs, scratch, _ = (
        (first_kernel, [tall, square, tall, tall, square], [], "pivot_first")
        if panel == 0
        else (
            next_kernel,
            [tall, tall, square],
            [
                pltpu.VMEM((rows, PANEL), jnp.bfloat16),
                pltpu.VMEM((PANEL, PANEL), jnp.float32),
                pltpu.VMEM((PANEL, PANEL), jnp.float32),
            ],
            "pivot_next",
        )
    )
    scratch = [
        pltpu.VMEM((own_arcs * len(basis), local, capacity), jnp.bfloat16),
        pltpu.VMEM((own_arcs * len(basis), capacity, local), jnp.bfloat16),
    ] + scratch
    args = (values[None, :], *basis, *pieces, *prior)
    return pl.pallas_call(
        functools.partial(kernel, len(basis), len(pieces), layout),
        out_shape=outs,
        in_specs=[pl.BlockSpec(memory_space=pltpu.SMEM)] + [vmem] * len(args),
        out_specs=[vmem] * len(outs),
        scratch_shapes=scratch,
        compiler_params=pltpu.CompilerParams(vmem_limit_bytes=56 << 20),
    )(table, *args)


def assemble_kernel(spec, table_ref, own_ref, *refs):
    arcs, own_arcs, pieces, layout = spec
    got_refs, refs = refs[: arcs - 1], refs[arcs - 1 :]
    tile_refs, refs = refs[:pieces], refs[pieces:]
    moved, refs = refs[:arcs], refs[arcs:]
    top0, top1, rest0, rest1, md0, md1, d_ref, normal_ref, panel_ref = refs[:9]
    basis_ref, turned_ref, xc, xct, xr, xrt, fr_top, fr_rest, fc_top, fc_rest, work = refs[9:]
    width, tile_rows = xc.shape[1], xr.shape[1]
    total_rows = xc.shape[0]
    row_start = table_ref[0]
    tile_start = table_ref[1] + pl.program_id(0) * width
    chunk = min(CHUNK, tile_rows, width)

    def turn(source, target):
        for at in range(0, total_rows, LANES):
            target[:, at : at + LANES] = source[at : at + LANES, :].T

    def factor(xt_ref, at, start):
        xt = xt_ref[at, :]
        for panel, (top, rest) in enumerate(((top0, rest0), (top1, rest1))):
            to = slice(panel * PANEL, (panel + 1) * PANEL)
            work[:, to] = product(xt, top[...], ((1,), (0,))) + product(xt, rest[...], ((1,), (0,)))
        for panel, md in enumerate((md0, md1)):
            to = slice(panel * PANEL, (panel + 1) * PANEL)

            @pl.when((start >= panel * PANEL) & (start < (panel + 1) * PANEL))
            def _(to=to, md=md, panel=panel):
                off = pl.multiple_of(start - panel * PANEL, chunk)
                work[:, to] = work[:, to] + md[pl.ds(off, chunk), :]

            @pl.when(start < panel * PANEL)
            def _(to=to):
                work[:, to] = jnp.zeros((chunk, PANEL), jnp.float32)

    @pl.when(pl.program_id(0) == 0)
    def _():
        turn_bases(moved, basis_ref, turned_ref)
        clean_pieces(tile_refs, layout, table_ref, 2, basis_ref, turned_ref, xr)
        turn(xr, xrt)

        def row_chunk(i, carry):
            at = pl.ds(pl.multiple_of(i * chunk, chunk), chunk)
            factor(xrt, at, row_start + i * chunk)
            fr_top[at, :], fr_rest[at, :] = split(work[...])
            return carry

        lax.fori_loop(0, tile_rows // chunk, row_chunk, 0)

    columns = [((s,), a) for s in range(arcs) for a in range(own_arcs)]
    clean_pieces(
        [own_ref, *got_refs], columns, table_ref, 2 + 3 * len(layout), basis_ref, turned_ref, xc
    )
    turn(xc, xct)

    def col_chunk(i, carry):
        at = pl.ds(pl.multiple_of(i * chunk, chunk), chunk)
        factor(xct, at, tile_start + i * chunk)
        for panel in range(PANELS):
            panel_ref[panel, at, :] = work[:, panel * PANEL : (panel + 1) * PANEL]
        fc_top[at, :], fc_rest[at, :] = split(work[...])
        return carry

    lax.fori_loop(0, width // chunk, col_chunk, 0)
    d = d_ref[:, pl.ds(pl.multiple_of(jnp.clip(tile_start - row_start, 0, tile_rows - width), LANES), width)]

    def normal_chunk(i, carry):
        at = pl.ds(pl.multiple_of(i * chunk, chunk), chunk)
        dims = ((1,), (1,))
        value = product(xrt[at, :], xc[...], ((1,), (0,))) - (
            product(fr_top[at, :], fc_top[...], dims)
            + (product(fr_top[at, :], fc_rest[...], dims) + product(fr_rest[at, :], fc_top[...], dims))
        )
        row = lax.broadcasted_iota(jnp.int32, (chunk, width), 0) + (row_start + i * chunk)
        col = lax.broadcasted_iota(jnp.int32, (chunk, width), 1) + tile_start
        normal_ref[at, :] = value + jnp.where(row == col, d, 0.0)
        return carry

    lax.fori_loop(0, tile_rows // chunk, normal_chunk, 0)


def assemble(own, got, tiles, layout, basis, tops, rests, mds, regularizer, table, own_arcs):
    arcs = len(got) + 1
    rows = own.shape[0] * arcs
    col_width, tile_rows = own.shape[1], regularizer.shape[0]
    width = min(512 if rows <= 2048 else 256, col_width, tile_rows)
    depth = PANEL * PANELS
    chunk = min(CHUNK, tile_rows, width)
    once = pl.Buffered(1)

    def whole(array):
        zeros = (0,) * array.ndim
        return pl.BlockSpec(array.shape, lambda s, t: zeros, pipeline_mode=once)

    fixed = [*tiles, *basis, *tops, *rests, *mds, regularizer[None, :]]
    columns = pl.BlockSpec((own.shape[0], width), lambda s, t: (0, s))
    return pl.pallas_call(
        functools.partial(assemble_kernel, (arcs, own_arcs, len(tiles), layout)),
        out_shape=(
            jax.ShapeDtypeStruct((tile_rows, col_width), jnp.float32),
            jax.ShapeDtypeStruct((PANELS, col_width, PANEL), jnp.float32),
        ),
        grid_spec=pltpu.PrefetchScalarGridSpec(
            num_scalar_prefetch=1,
            grid=(col_width // width,),
            in_specs=[columns] * arcs + [whole(array) for array in fixed],
            out_specs=(
                pl.BlockSpec((tile_rows, width), lambda s, t: (0, s)),
                pl.BlockSpec((PANELS, width, PANEL), lambda s, t: (0, s, 0)),
            ),
            scratch_shapes=[
                pltpu.VMEM((own_arcs * arcs, *basis[0].shape[1:]), jnp.bfloat16),
                pltpu.VMEM((own_arcs * arcs, *basis[0].shape[:0:-1]), jnp.bfloat16),
                pltpu.VMEM((rows, width), jnp.bfloat16),
                pltpu.VMEM((width, rows), jnp.bfloat16),
                pltpu.VMEM((rows, tile_rows), jnp.bfloat16),
                pltpu.VMEM((tile_rows, rows), jnp.bfloat16),
                pltpu.VMEM((tile_rows, depth), jnp.bfloat16),
                pltpu.VMEM((tile_rows, depth), jnp.bfloat16),
                pltpu.VMEM((width, depth), jnp.bfloat16),
                pltpu.VMEM((width, depth), jnp.bfloat16),
                pltpu.VMEM((chunk, depth), jnp.float32),
            ],
        ),
        compiler_params=pltpu.CompilerParams(vmem_limit_bytes=60 << 20),
        name="assemble",
    )(table, own, *got, *fixed)


def per_device(plan, design, local_design, lengths, regularizer):
    row_count, col_width = design.shape
    tile_rows = regularizer.shape[0]
    own_arcs = lengths.shape[0]
    capacity = row_count // own_arcs
    half_arcs = own_arcs // CORES
    arc_index, trow_index = lax.axis_index("arc"), lax.axis_index("trow")
    tcol_index = lax.axis_index("tcol")
    core, x_index = tcol_index % CORES, tcol_index // CORES
    row_start = (arc_index * plan.trow + trow_index) * tile_rows
    col_start = tcol_index * col_width
    lead = PANEL * PANELS

    live_rows = jnp.arange(capacity, dtype=jnp.int32)[None, :] < lengths[:, None]
    live_flat = live_rows.reshape(row_count, 1)
    zero = jnp.zeros((), design.dtype)

    def arc_back(s):
        return lax.rem(arc_index + plan.arc - s, plan.arc)

    def half_entries(halves_count):
        layout, entries = [], []
        for n, which in enumerate((core, 1 - core)):
            for s in range(plan.arc):
                for a in range(half_arcs):
                    offset = which * half_arcs + a
                    layout.append(((n * halves_count + s,), a))
                    entries += [arc_back(s) * own_arcs + offset, s * own_arcs + offset, 0]
        return layout, entries

    def from_lead(arc, trow, tcol):
        return tcol < CORES

    def spread_lead(mine, source):
        return [
            [
                plan.move(mine, s, dx, source) if s or dx else mine
                for dx in range(plan.across)
            ]
            for s in range(plan.arc)
        ]

    def lead_block(panel, live):
        return jnp.where(live, design[:, panel * PANEL : (panel + 1) * PANEL], zero)

    mine = plan.own_half(lead_block(0, live_flat), 0)
    halves = []
    for arrived in spread_lead(mine, None):
        best = arrived[0]
        for dx in range(1, plan.across):
            best = jnp.where(x_index == dx, arrived[dx], best)
        halves.append(best)
    first_pieces = halves + [plan.core_swap(half) for half in halves]

    live_rows, local_design = lax.optimization_barrier((live_rows, local_design, mine))[:2]
    local_half = local_design.reshape(own_arcs, capacity, -1)
    local_half = jnp.where(live_rows[:, :, None], local_half, jnp.zeros((), local_design.dtype))
    basis_own = local_basis(local_half)
    basis = [basis_own] + [plan.move(basis_own, s, 0) for s in range(1, plan.arc)]

    live_flat = after(live_flat, basis_own)
    block = lead_block(1, live_flat)
    mine = jnp.where(core == 0, block, plan.core_swap(block))
    arrivals = spread_lead(mine, from_lead)
    next_pieces = [got for arrived in arrivals for got in arrived]
    next_layout = [
        (tuple(s * plan.across + dx for dx in range(plan.across)), a)
        for s in range(plan.arc)
        for a in range(own_arcs)
    ]
    live_flat = after(live_flat, mine)

    masked = jnp.where(live_flat, design, zero)
    got_columns = [plan.move(masked, s, 0) for s in range(1, plan.arc)]

    def holder(a, r):
        return (a % plan.arc * plan.trow + r) * tile_rows // col_width

    my_holder = row_start // col_width
    halves = []
    for s in range(plan.arc):
        target = (lax.rem(arc_index + s, plan.arc) * plan.trow + trow_index) * tile_rows
        tile = lax.dynamic_slice_in_dim(masked, lax.rem(target, col_width), tile_rows, 1)
        mine = plan.own_half(tile, target // col_width % CORES)

        def has_tile(a, r, c, s=s):
            return holder(a + s, r) // CORES == c // CORES

        arrived = [
            plan.move(mine, s, dx, has_tile if s else None) if s or dx else mine
            for dx in range(plan.across)
        ]
        best = arrived[0]
        for dx in range(1, plan.across):
            far = lax.rem(x_index + plan.across - my_holder // CORES, plan.across) == dx
            best = jnp.where(far, arrived[dx], best)
        halves.append(best)

    lead_tiles = -(-lead // tile_rows)
    all_regularizer = plan.gather_rows(regularizer)[: lead_tiles * tile_rows][:lead]

    def table_of(*values):
        return jnp.stack([jnp.asarray(v, jnp.int32) for v in values])

    layout, entries = half_entries(plan.arc)
    first_rows, prior, *first_parts = pivot_call(
        0, layout, table_of(*entries), all_regularizer[:PANEL], basis, first_pieces, ()
    )

    def arc_entries(chosen):
        return [
            v
            for s in range(plan.arc)
            for a in range(own_arcs)
            for v in (arc_back(s) * own_arcs + a, s * own_arcs + a, chosen)
        ]

    next_parts = pivot_call(
        1,
        next_layout,
        table_of(*arc_entries(x_index)),
        all_regularizer[PANEL:lead],
        basis,
        next_pieces,
        (first_rows, prior),
    )
    tiles = halves + [plan.core_swap(half) for half in halves]
    return assemble(
        masked,
        got_columns,
        tiles,
        layout,
        basis,
        *[[a, b] for a, b in zip(first_parts, next_parts)],
        regularizer,
        table_of(row_start, col_start, *entries, *arc_entries(0)),
        own_arcs,
    )


def solution(mesh):
    plan = Plan(mesh)

    def body(*args):
        return per_device(plan, *args)

    return jax.shard_map(
        body,
        mesh=mesh,
        in_specs=(P("arc", "tcol"), P("arc", None), P("arc"), P(("arc", "trow"))),
        out_specs=(P(("arc", "trow"), "tcol"), P(None, "tcol", None)),
        check_vma=False,
    )
```

```python
import functools

import jax
import jax.numpy as jnp
from jax import lax
from jax.experimental import pallas as pl
from jax.experimental.pallas import tpu as pltpu
from jax.sharding import PartitionSpec as P

PANEL = 512
PANELS = 2
AXES = ("arc", "trow", "tcol")
CORES = 2


ridge = 0.1

HIGHEST = lax.Precision.HIGHEST
LANES = 128
CHUNK = 512
SUB = 8


def inverse_factor(rows):
    groups = LANES // SUB
    rows = list(rows)
    lane = lax.broadcasted_iota(jnp.int32, (SUB, LANES), 1)
    sub = lax.broadcasted_iota(jnp.int32, (SUB, LANES), 0)
    shape = (SUB, LANES)
    out = []
    for s in range(groups):
        j = s * SUB
        inside = (lane >= j) & (lane < j + SUB)
        lead = rows[s]
        merged = jnp.where(inside, jnp.where(lane == sub + j, 1.0, 0.0), lead)
        z = [jnp.broadcast_to(merged[k : k + 1, :], shape) for k in range(SUB)]
        sp = {
            (m, k): jnp.broadcast_to(lead[k : k + 1, j + m : j + m + 1], shape)
            for k in range(SUB)
            for m in range(k, SUB)
        }
        below = range(s + 1, groups)
        col = {
            (t, k): jnp.broadcast_to(rows[t][:, j + k : j + k + 1], shape)
            for t in below
            for k in range(SUB)
        }
        rest = {t: jnp.where(inside, 0.0, rows[t]) for t in below}
        soon = below[:1]
        factor, inverses = {}, {}
        for k in range(0, SUB, 2):
            a, b, c = sp[k, k], sp[k + 1, k], sp[k + 1, k + 1]
            det = a * c - b * b
            root = lax.rsqrt(det)
            scale = root * root
            pair = {
                m: (c * sp[m, k] - b * sp[m, k + 1], a * sp[m, k + 1] - b * sp[m, k])
                for m in range(k + 2, SUB)
            }
            first = lax.rsqrt(a)
            second = root * (a * first)
            one = {m: sp[m, k] * first for m in range(k + 1, SUB)}
            two = {m: (sp[m, k + 1] - one[k + 1] * one[m]) * second for m in range(k + 2, SUB)}
            for m in range(k + 2, SUB):
                for n in range(m, SUB):
                    sp[n, m] = sp[n, m] - (sp[n, k] * pair[m][0] + sp[n, k + 1] * pair[m][1]) * scale
            for at, inv, l in ((k, first, one), (k + 1, second, two)):
                factor[at], inverses[at] = l, inv
                z[at] = z[at] * inv
                for m in range(at + 1, SUB):
                    z[m] = z[m] - l[m] * z[at]
                for t in soon:
                    coef = col[t, at] * inv
                    for m in range(at + 1, SUB):
                        col[t, m] = col[t, m] - coef * l[m]
                    rest[t] = rest[t] - coef * z[at]
        back = {}
        for k in reversed(range(SUB)):
            back[k] = z[k]
            for m in range(k + 1, SUB):
                back[k] = back[k] - factor[k][m] * back[m]
            back[k] = back[k] * inverses[k]
        for t in below:
            if t not in soon:
                for k in range(SUB):
                    rest[t] = rest[t] - col[t, k] * back[k]
            rows[t] = rest[t]
        done = z[0]
        for k in range(1, SUB):
            done = jnp.where(sub == k, z[k], done)
        out.append(jnp.where(lane <= sub + j, done, 0.0))
    return out


def rows_of(block):
    return [block[SUB * t:SUB * (t + 1), :] for t in range(LANES // SUB)]


class Plan:
    def __init__(self, mesh):
        self.arc, self.trow, self.tcol = (mesh.shape[name] for name in AXES)
        self.across = self.tcol // CORES

    def flat(self, arc, trow, tcol):
        return (arc % self.arc * self.trow + trow) * self.tcol + tcol % self.tcol

    def move(self, block, arcs, across, source=None):
        pairs = [
            (self.flat(a, r, c), self.flat(a + arcs, r, c + across * CORES))
            for a in range(self.arc)
            for r in range(self.trow)
            for c in range(self.tcol)
            if source is None or source(a, r, c)
        ]
        return lax.ppermute(block, AXES, pairs)

    def core_swap(self, block):
        pairs = [
            (self.flat(a, r, c), self.flat(a, r, c ^ 1))
            for a in range(self.arc)
            for r in range(self.trow)
            for c in range(self.tcol)
        ]
        return lax.ppermute(block, AXES, pairs)

    def own_half(self, block, holder_core):
        half = block.shape[0] // CORES
        core = lax.axis_index("tcol") % CORES
        got = self.core_swap(block)
        mine = lax.dynamic_slice_in_dim(block, core * half, half, 0)
        theirs = lax.dynamic_slice_in_dim(got, core * half, half, 0)
        return jnp.where(core == holder_core, mine, theirs)

    def gather_rows(self, tile):
        me = lax.axis_index("arc") * self.trow + lax.axis_index("trow")
        total = self.arc * self.trow
        spans = [self.trow << n for n in range(self.arc.bit_length() - 1)]
        spans += [1 << n for n in range(self.trow.bit_length() - 1)]
        tile = tile[None]
        for span in spans:
            pairs = [
                (t * self.tcol + c, (t ^ span) * self.tcol + c)
                for t in range(total)
                for c in range(self.tcol)
            ]
            got = lax.ppermute(tile, AXES, pairs)
            low = (me & span) == 0
            tile = jnp.concatenate([jnp.where(low, tile, got), jnp.where(low, got, tile)])
        blocks = tile.reshape(self.trow, self.arc, -1)
        return jnp.transpose(blocks, (1, 0, 2)).reshape(-1)


def local_kernel(a_ref, n_ref):
    n_ref[0] = jnp.concatenate(inverse_factor(rows_of(a_ref[0])), axis=0)


def local_call(a):
    block = pl.BlockSpec((1,) + a.shape[1:], lambda i: (i, 0, 0))
    return pl.pallas_call(
        local_kernel,
        out_shape=jax.ShapeDtypeStruct(a.shape, jnp.float32),
        grid=(a.shape[0],),
        in_specs=[block],
        out_specs=block,
        name="local_inverse",
    )(a)


def local_basis(local_half):
    local_normal = jnp.einsum(
        "acl,acm->alm", local_half, local_half, preferred_element_type=jnp.float32
    )
    local_normal = local_normal + ridge * jnp.eye(local_half.shape[2], dtype=jnp.float32)[None]
    inverse = local_call(local_normal)
    basis_rows = jnp.einsum(
        "alm,acm->alc", inverse, local_half.astype(jnp.float32), precision=HIGHEST
    )
    return basis_rows.astype(jnp.bfloat16)


def after(value, *earlier):
    return lax.optimization_barrier((value,) + earlier)[0]


def product(left, right, dims, precision=None):
    return lax.dot_general(
        left, right, (dims, ((), ())), precision=precision, preferred_element_type=jnp.float32
    )


def fine(left, right, dims):
    left_top, right_top = left.astype(jnp.bfloat16), right.astype(jnp.bfloat16)
    left_rest = (left - left_top.astype(jnp.float32)).astype(jnp.bfloat16)
    right_rest = (right - right_top.astype(jnp.float32)).astype(jnp.bfloat16)
    return product(left_top, right_top, dims) + (
        product(left_top, right_rest, dims) + product(left_rest, right_top, dims)
    )


def eliminate(m_ref):
    n = m_ref.shape[0]
    blocks = n // LANES
    row = lax.broadcasted_iota(jnp.int32, (LANES, LANES), 0)
    col = lax.broadcasted_iota(jnp.int32, (LANES, LANES), 1)

    def step(i, carry):
        at = pl.ds(pl.multiple_of(i * LANES, LANES), LANES)
        inv = jnp.concatenate(inverse_factor(rows_of(m_ref[at, at])), axis=0)
        m_ref[at, at] = jnp.where(row == col, 1.0, 0.0)
        m_ref[at, :] = fine(inv, m_ref[at, :], ((1,), (0,)))

        def update(t, carry):
            to = pl.ds(pl.multiple_of(t * LANES, LANES), LANES)
            coef = m_ref[at, to]
            m_ref[to, at] = jnp.zeros((LANES, LANES), jnp.float32)
            m_ref[to, :] = m_ref[to, :] - fine(coef, m_ref[at, :], ((0,), (0,)))
            return carry

        lax.fori_loop(i + 1, blocks, update, 0)
        kept = lax.broadcasted_iota(jnp.int32, (LANES, n), 1) < (i + 1) * LANES
        m_ref[at, :] = jnp.where(kept, m_ref[at, :], 0.0)
        return carry

    lax.fori_loop(0, blocks, step, 0)


def on_diagonal(values, n):
    row = lax.broadcasted_iota(jnp.int32, (n, n), 0)
    col = lax.broadcasted_iota(jnp.int32, (n, n), 1)
    return jnp.where(row == col, values, 0.0)


def clean(block, basis, turned):
    loadings = product(basis, block, ((1,), (0,))).astype(jnp.bfloat16)
    return (block.astype(jnp.float32) - product(turned, loadings, ((1,), (0,)))).astype(
        jnp.bfloat16
    )


def clean_pieces(choices, layout, table_ref, base, basis_ref, turned_ref, out_ref):
    capacity = basis_ref.shape[2]
    for n, (candidates, at) in enumerate(layout):
        slot, rel, chosen = (table_ref[base + 3 * n + i] for i in range(3))
        to = pl.ds(pl.multiple_of(slot * capacity, 64), capacity)
        rows = slice(at * capacity, (at + 1) * capacity)

        def put(ref, to=to, rows=rows, rel=rel):
            out_ref[to, :] = clean(ref[rows, :], basis_ref[rel], turned_ref[rel])

        if len(candidates) == 1:
            put(choices[candidates[0]])
            continue
        for which, candidate in enumerate(candidates):

            @pl.when(chosen == which)
            def _(put=put, candidate=candidate):
                put(choices[candidate])


def turn_bases(moved_refs, basis_ref, turned_ref):
    for s, moved in enumerate(moved_refs):
        for a in range(moved.shape[0]):
            basis_ref[s * moved.shape[0] + a] = moved[a]
            turned_ref[s * moved.shape[0] + a] = moved[a].T


def split(value):
    top = value.astype(jnp.bfloat16)
    return top, (value - top.astype(jnp.float32)).astype(jnp.bfloat16)


def weigh(terms, top_ref, rest_ref):
    rows = top_ref.shape[0]
    chunk = next(n for n in (640, 512, 320, 256, LANES, SUB) if rows % n == 0 and rows > n)
    parts = [(ref, *split(factor)) for ref, factor in terms]

    def step(i, carry):
        at = pl.ds(pl.multiple_of(i * chunk, chunk), chunk)
        total = None
        for ref, top, rest in parts:
            x = ref[at, :]
            term = product(x, top, ((1,), (1,))) + product(x, rest, ((1,), (1,)))
            total = term if total is None else total + term
        top_ref[at, :], rest_ref[at, :] = split(total)
        return carry

    lax.fori_loop(0, rows // chunk, step, 0)


def first_kernel(arcs, pieces, layout, table_ref, d_ref, *refs):
    moved, refs = refs[:arcs], refs[arcs:]
    piece_refs = refs[:pieces]
    x_ref, m_ref, top_ref, rest_ref, md_ref, basis_ref, turned_ref = refs[pieces:]
    turn_bases(moved, basis_ref, turned_ref)
    n = m_ref.shape[0]
    clean_pieces(piece_refs, layout, table_ref, 0, basis_ref, turned_ref, x_ref)
    x = x_ref[...]
    m_ref[...] = product(x, x, ((0,), (0,))) + on_diagonal(d_ref[...], n)
    eliminate(m_ref)
    inverse = m_ref[...]
    weigh([(x_ref, inverse)], top_ref, rest_ref)
    md_ref[...] = (inverse * d_ref[...]).T


def next_kernel(arcs, pieces, layout, table_ref, d_ref, *refs):
    moved, refs = refs[:arcs], refs[arcs:]
    piece_refs, refs = refs[:pieces], refs[pieces:]
    before_ref, prior_ref, top_ref, rest_ref, md_ref = refs[:5]
    basis_ref, turned_ref, x_ref, m_ref, cross_ref = refs[5:]
    turn_bases(moved, basis_ref, turned_ref)
    n = m_ref.shape[0]
    clean_pieces(piece_refs, layout, table_ref, 0, basis_ref, turned_ref, x_ref)
    x = x_ref[...]
    cross = fine(prior_ref[...], product(before_ref[...], x, ((0,), (0,))), ((1,), (0,)))
    m_ref[...] = product(x, x, ((0,), (0,))) + on_diagonal(d_ref[...], n) - fine(
        cross, cross, ((0,), (0,))
    )
    cross_ref[...] = fine(cross, prior_ref[...], ((0,), (0,)))
    eliminate(m_ref)
    inverse = m_ref[...]
    back = -fine(inverse, cross_ref[...], ((1,), (0,)))
    weigh([(x_ref, inverse), (before_ref, back)], top_ref, rest_ref)
    md_ref[...] = (inverse * d_ref[...]).T


def pivot_call(panel, layout, table, values, basis, pieces, prior):
    own_arcs, local, capacity = basis[0].shape
    rows = own_arcs * len(basis) * capacity
    square = jax.ShapeDtypeStruct((PANEL, PANEL), jnp.float32)
    tall = jax.ShapeDtypeStruct((rows, PANEL), jnp.bfloat16)
    vmem = pl.BlockSpec(memory_space=pltpu.VMEM)
    kernel, outs, scratch, _ = (
        (first_kernel, [tall, square, tall, tall, square], [], "pivot_first")
        if panel == 0
        else (
            next_kernel,
            [tall, tall, square],
            [
                pltpu.VMEM((rows, PANEL), jnp.bfloat16),
                pltpu.VMEM((PANEL, PANEL), jnp.float32),
                pltpu.VMEM((PANEL, PANEL), jnp.float32),
            ],
            "pivot_next",
        )
    )
    scratch = [
        pltpu.VMEM((own_arcs * len(basis), local, capacity), jnp.bfloat16),
        pltpu.VMEM((own_arcs * len(basis), capacity, local), jnp.bfloat16),
    ] + scratch
    args = (values[None, :], *basis, *pieces, *prior)
    return pl.pallas_call(
        functools.partial(kernel, len(basis), len(pieces), layout),
        out_shape=outs,
        in_specs=[pl.BlockSpec(memory_space=pltpu.SMEM)] + [vmem] * len(args),
        out_specs=[vmem] * len(outs),
        scratch_shapes=scratch,
        compiler_params=pltpu.CompilerParams(vmem_limit_bytes=56 << 20),
    )(table, *args)


def assemble_kernel(spec, table_ref, own_ref, *refs):
    arcs, own_arcs, pieces, layout = spec
    got_refs, refs = refs[: arcs - 1], refs[arcs - 1 :]
    tile_refs, refs = refs[:pieces], refs[pieces:]
    moved, refs = refs[:arcs], refs[arcs:]
    top0, top1, rest0, rest1, md0, md1, d_ref, normal_ref, panel_ref = refs[:9]
    basis_ref, turned_ref, xc, xct, xr, xrt, fr_top, fr_rest, fc_top, fc_rest, work = refs[9:]
    width, tile_rows = xc.shape[1], xr.shape[1]
    total_rows = xc.shape[0]
    row_start = table_ref[0]
    tile_start = table_ref[1] + pl.program_id(0) * width
    chunk = min(CHUNK, tile_rows, width)

    def turn(source, target):
        for at in range(0, total_rows, LANES):
            target[:, at : at + LANES] = source[at : at + LANES, :].T

    def factor(xt_ref, at, start):
        xt = xt_ref[at, :]
        for panel, (top, rest) in enumerate(((top0, rest0), (top1, rest1))):
            to = slice(panel * PANEL, (panel + 1) * PANEL)
            work[:, to] = product(xt, top[...], ((1,), (0,))) + product(xt, rest[...], ((1,), (0,)))
        for panel, md in enumerate((md0, md1)):
            to = slice(panel * PANEL, (panel + 1) * PANEL)

            @pl.when((start >= panel * PANEL) & (start < (panel + 1) * PANEL))
            def _(to=to, md=md, panel=panel):
                off = pl.multiple_of(start - panel * PANEL, chunk)
                work[:, to] = work[:, to] + md[pl.ds(off, chunk), :]

            @pl.when(start < panel * PANEL)
            def _(to=to):
                work[:, to] = jnp.zeros((chunk, PANEL), jnp.float32)

    @pl.when(pl.program_id(0) == 0)
    def _():
        turn_bases(moved, basis_ref, turned_ref)
        clean_pieces(tile_refs, layout, table_ref, 2, basis_ref, turned_ref, xr)
        turn(xr, xrt)

        def row_chunk(i, carry):
            at = pl.ds(pl.multiple_of(i * chunk, chunk), chunk)
            factor(xrt, at, row_start + i * chunk)
            fr_top[at, :], fr_rest[at, :] = split(work[...])
            return carry

        lax.fori_loop(0, tile_rows // chunk, row_chunk, 0)

    columns = [((s,), a) for s in range(arcs) for a in range(own_arcs)]
    clean_pieces(
        [own_ref, *got_refs], columns, table_ref, 2 + 3 * len(layout), basis_ref, turned_ref, xc
    )
    turn(xc, xct)

    def col_chunk(i, carry):
        at = pl.ds(pl.multiple_of(i * chunk, chunk), chunk)
        factor(xct, at, tile_start + i * chunk)
        for panel in range(PANELS):
            panel_ref[panel, at, :] = work[:, panel * PANEL : (panel + 1) * PANEL]
        fc_top[at, :], fc_rest[at, :] = split(work[...])
        return carry

    lax.fori_loop(0, width // chunk, col_chunk, 0)
    d = d_ref[:, pl.ds(pl.multiple_of(jnp.clip(tile_start - row_start, 0, tile_rows - width), LANES), width)]

    tall = min(2 * CHUNK, tile_rows)

    def normal_chunk(i, carry):
        at = pl.ds(pl.multiple_of(i * tall, tall), tall)
        dims = ((1,), (1,))
        value = product(xrt[at, :], xc[...], ((1,), (0,))) - (
            product(fr_top[at, :], fc_top[...], dims)
            + (product(fr_top[at, :], fc_rest[...], dims) + product(fr_rest[at, :], fc_top[...], dims))
        )
        row = lax.broadcasted_iota(jnp.int32, (tall, width), 0) + (row_start + i * tall)
        col = lax.broadcasted_iota(jnp.int32, (tall, width), 1) + tile_start
        normal_ref[at, :] = value + jnp.where(row == col, d, 0.0)
        return carry

    lax.fori_loop(0, tile_rows // tall, normal_chunk, 0)


def assemble(own, got, tiles, layout, basis, tops, rests, mds, regularizer, table, own_arcs):
    arcs = len(got) + 1
    rows = own.shape[0] * arcs
    col_width, tile_rows = own.shape[1], regularizer.shape[0]
    width = min(512 if rows <= 2048 else 256, col_width, tile_rows)
    depth = PANEL * PANELS
    chunk = min(CHUNK, tile_rows, width)
    once = pl.Buffered(1)

    def whole(array):
        zeros = (0,) * array.ndim
        return pl.BlockSpec(array.shape, lambda s, t: zeros, pipeline_mode=once)

    fixed = [*tiles, *basis, *tops, *rests, *mds, regularizer[None, :]]
    columns = pl.BlockSpec((own.shape[0], width), lambda s, t: (0, s))
    return pl.pallas_call(
        functools.partial(assemble_kernel, (arcs, own_arcs, len(tiles), layout)),
        out_shape=(
            jax.ShapeDtypeStruct((tile_rows, col_width), jnp.float32),
            jax.ShapeDtypeStruct((PANELS, col_width, PANEL), jnp.float32),
        ),
        grid_spec=pltpu.PrefetchScalarGridSpec(
            num_scalar_prefetch=1,
            grid=(col_width // width,),
            in_specs=[columns] * arcs + [whole(array) for array in fixed],
            out_specs=(
                pl.BlockSpec((tile_rows, width), lambda s, t: (0, s)),
                pl.BlockSpec((PANELS, width, PANEL), lambda s, t: (0, s, 0)),
            ),
            scratch_shapes=[
                pltpu.VMEM((own_arcs * arcs, *basis[0].shape[1:]), jnp.bfloat16),
                pltpu.VMEM((own_arcs * arcs, *basis[0].shape[:0:-1]), jnp.bfloat16),
                pltpu.VMEM((rows, width), jnp.bfloat16),
                pltpu.VMEM((width, rows), jnp.bfloat16),
                pltpu.VMEM((rows, tile_rows), jnp.bfloat16),
                pltpu.VMEM((tile_rows, rows), jnp.bfloat16),
                pltpu.VMEM((tile_rows, depth), jnp.bfloat16),
                pltpu.VMEM((tile_rows, depth), jnp.bfloat16),
                pltpu.VMEM((width, depth), jnp.bfloat16),
                pltpu.VMEM((width, depth), jnp.bfloat16),
                pltpu.VMEM((chunk, depth), jnp.float32),
            ],
        ),
        compiler_params=pltpu.CompilerParams(vmem_limit_bytes=60 << 20),
        name="assemble",
    )(table, own, *got, *fixed)


def per_device(plan, design, local_design, lengths, regularizer):
    row_count, col_width = design.shape
    tile_rows = regularizer.shape[0]
    own_arcs = lengths.shape[0]
    capacity = row_count // own_arcs
    half_arcs = own_arcs // CORES
    arc_index, trow_index = lax.axis_index("arc"), lax.axis_index("trow")
    tcol_index = lax.axis_index("tcol")
    core, x_index = tcol_index % CORES, tcol_index // CORES
    row_start = (arc_index * plan.trow + trow_index) * tile_rows
    col_start = tcol_index * col_width
    lead = PANEL * PANELS

    live_rows = jnp.arange(capacity, dtype=jnp.int32)[None, :] < lengths[:, None]
    live_flat = live_rows.reshape(row_count, 1)
    zero = jnp.zeros((), design.dtype)

    def arc_back(s):
        return lax.rem(arc_index + plan.arc - s, plan.arc)

    def half_entries(halves_count):
        layout, entries = [], []
        for n, which in enumerate((core, 1 - core)):
            for s in range(plan.arc):
                for a in range(half_arcs):
                    offset = which * half_arcs + a
                    layout.append(((n * halves_count + s,), a))
                    entries += [arc_back(s) * own_arcs + offset, s * own_arcs + offset, 0]
        return layout, entries

    def from_lead(arc, trow, tcol):
        return tcol < CORES

    def spread_lead(mine, source):
        return [
            [
                plan.move(mine, s, dx, source if s else None) if s or dx else mine
                for dx in range(plan.across)
            ]
            for s in range(plan.arc)
        ]

    def lead_block(panel, live):
        return jnp.where(live, design[:, panel * PANEL : (panel + 1) * PANEL], zero)

    mine = plan.own_half(lead_block(0, live_flat), 0)
    halves = []
    for arrived in spread_lead(mine, None):
        best = arrived[0]
        for dx in range(1, plan.across):
            best = jnp.where(x_index == dx, arrived[dx], best)
        halves.append(best)
    first_pieces = halves + [plan.core_swap(half) for half in halves]

    live_rows, local_design = lax.optimization_barrier((live_rows, local_design, mine))[:2]
    local_half = local_design.reshape(own_arcs, capacity, -1)
    local_half = jnp.where(live_rows[:, :, None], local_half, jnp.zeros((), local_design.dtype))
    basis_own = local_basis(local_half)
    basis = [basis_own] + [plan.move(basis_own, s, 0) for s in range(1, plan.arc)]

    live_flat = after(live_flat, basis_own)
    block = lead_block(1, live_flat)
    mine = jnp.where(core == 0, block, plan.core_swap(block))
    arrivals = spread_lead(mine, from_lead)
    next_pieces = [got for arrived in arrivals for got in arrived]
    next_layout = [
        (tuple(s * plan.across + dx for dx in range(plan.across)), a)
        for s in range(plan.arc)
        for a in range(own_arcs)
    ]
    live_flat = after(live_flat, mine)

    masked = jnp.where(live_flat, design, zero)
    got_columns = [plan.move(masked, s, 0) for s in range(1, plan.arc)]

    def holder(a, r):
        return (a % plan.arc * plan.trow + r) * tile_rows // col_width

    my_holder = row_start // col_width
    halves = []
    for s in range(plan.arc):
        target = (lax.rem(arc_index + s, plan.arc) * plan.trow + trow_index) * tile_rows
        tile = lax.dynamic_slice_in_dim(masked, lax.rem(target, col_width), tile_rows, 1)
        mine = plan.own_half(tile, target // col_width % CORES)

        def has_tile(a, r, c, s=s):
            return holder(a + s, r) // CORES == c // CORES

        arrived = [
            plan.move(mine, s, dx, has_tile if s else None) if s or dx else mine
            for dx in range(plan.across)
        ]
        best = arrived[0]
        for dx in range(1, plan.across):
            far = lax.rem(x_index + plan.across - my_holder // CORES, plan.across) == dx
            best = jnp.where(far, arrived[dx], best)
        halves.append(best)

    lead_tiles = -(-lead // tile_rows)
    all_regularizer = plan.gather_rows(regularizer)[: lead_tiles * tile_rows][:lead]

    def table_of(*values):
        return jnp.stack([jnp.asarray(v, jnp.int32) for v in values])

    layout, entries = half_entries(plan.arc)
    first_rows, prior, *first_parts = pivot_call(
        0, layout, table_of(*entries), all_regularizer[:PANEL], basis, first_pieces, ()
    )

    def arc_entries(chosen):
        return [
            v
            for s in range(plan.arc)
            for a in range(own_arcs)
            for v in (arc_back(s) * own_arcs + a, s * own_arcs + a, chosen)
        ]

    next_parts = pivot_call(
        1,
        next_layout,
        table_of(*arc_entries(x_index)),
        all_regularizer[PANEL:lead],
        basis,
        next_pieces,
        (first_rows, prior),
    )
    tiles = halves + [plan.core_swap(half) for half in halves]
    return assemble(
        masked,
        got_columns,
        tiles,
        layout,
        basis,
        *[[a, b] for a, b in zip(first_parts, next_parts)],
        regularizer,
        table_of(row_start, col_start, *entries, *arc_entries(0)),
        own_arcs,
    )


def solution(mesh):
    plan = Plan(mesh)

    def body(*args):
        return per_device(plan, *args)

    return jax.shard_map(
        body,
        mesh=mesh,
        in_specs=(P("arc", "tcol"), P("arc", None), P("arc"), P(("arc", "trow"))),
        out_specs=(P(("arc", "trow"), "tcol"), P(None, "tcol", None)),
        check_vma=False,
    )
```
